32 devices in a mesh: dp: 8 (over z, core), tensor: 4 (over y, x).
Axes of the slice: x: 2, y: 2, z: 4, core: 2. Of those that a mesh axis runs over, the one named last changes fastest.
Arguments:
- hidden_in: bfloat16 [2048, 8192], P(('dp', 'tensor')), may hold values from -6 to 6
- out_grad: bfloat16 [2048, 8192], P(('dp', 'tensor')), may hold values from -0.29882812 to 0.29882812
- seq_lengths: int32 [8, 8], P('dp'), may hold values from 1 to 128, 256 in all within a row
- seq_adapter: int32 [8, 8], P('dp'), may hold values from 0 to 15
- query_weight: bfloat16 [8192, 4096], P(None, 'tensor'), may hold values from -0.0625 to 0.0625
- key_value_weight: bfloat16 [2, 8192, 1024], P(None, None, 'tensor'), may hold values from -0.0625 to 0.0625
- output_weight: bfloat16 [4096, 8192], P('tensor'), may hold values from -0.09375 to 0.09375
- a_in: bfloat16 [16, 48, 8192], P('dp', None, 'tensor'), may hold values from -0.0625 to 0.0625
- b_query: bfloat16 [16, 16, 4096], P('dp', None, 'tensor'), may hold values from -0.375 to 0.375
- b_key_value: bfloat16 [16, 2, 16, 1024], P('dp', None, None, 'tensor'), may hold values from -0.375 to 0.375
- output_down_factor: bfloat16 [16, 16, 4096], P('dp', None, 'tensor'), may hold values from -0.09375 to 0.09375
- output_up_factor: bfloat16 [16, 16, 8192], P('dp', 'tensor'), may hold values from -0.375 to 0.375
Outputs:
- attn_out: bfloat16 [2048, 8192], P(('dp', 'tensor'))
- input_grad: bfloat16 [2048, 8192], P(('dp', 'tensor'))
- input_down_gradient: float32 [16, 48, 8192], P('dp', None, 'tensor')
- query_up_gradient: float32 [16, 16, 4096], P('dp', None, 'tensor')
- grad_b_key_value: float32 [16, 2, 16, 1024], P('dp', None, None, 'tensor')
- output_down_gradient: float32 [16, 16, 4096], P('dp', None, 'tensor')
- output_up_gradient: float32 [16, 16, 8192], P('dp', 'tensor')
The draws below stay inside these ranges and needn't reach their ends.
All inputs are finite; a program needn't handle non-finite values.
Results may differ from the reference program's by a relative error of at most 0.015.
Values may be sent and summed in bfloat16 or wider, within the bound.
A program may use at most 192 MiB of HBM per device.

```python
import math
import jax
import jax.numpy as jnp
import numpy as np
from jax import lax

MODEL_WIDTH = 8192
HQ = 32
KEY_VALUE_HEADS = 8
HEAD_SIZE = 128
ADAPTER_RANK = 16
GROUP_TOKENS = 256
NSEQ = 8
MOST = 128
ADAPTER_COUNT = 16
TOKENS = 2048
QW = 4096
KW = 1024
N_DP = 8
N_TENSOR = 4


def draw_hidden_in(key, part):
    values = jnp.clip(jax.random.normal(key, (TOKENS, MODEL_WIDTH), jnp.float32), -6.0, 6.0)
    return values.astype(jnp.bfloat16)


def touch_ends(entries, key, least, top_value):
    longest = entries.shape.index(max(entries.shape))
    spots = []
    for shift in (0, 1):
        where = [jax.random.randint(jax.random.fold_in(key, axis), (), 0, length) for axis, length in enumerate(entries.shape)]
        where[longest] = (where[longest] + shift) % entries.shape[longest]
        spots.append(tuple(where))
    return entries.at[spots[0]].set(least).at[spots[1]].set(top_value)


def block_levels(stream_key, dims, pieces, smallest, high):
    def one(dim, shards_of):
        heights = jax.random.uniform(jax.random.fold_in(jax.random.fold_in(stream_key, 6), dim), (shards_of,), jnp.float32, smallest / len(pieces), high / len(pieces))
        return jnp.repeat(jnp.exp(heights), dims[dim] // shards_of).reshape((-1,) + (1,) * (len(dims) - dim - 1))

    level = one(*pieces[0])
    for cut in pieces[1:]:
        level = level * one(*cut)
    return level


def profile(count, total, most, slope):
    portions = [(1 << 20) // math.isqrt(standing ** slope) + 1 for standing in range(2, count + 1)]
    rest, holding = total - most - (count - 1), [1] * (count - 1)
    while rest > 0:
        movable = [i for i in range(count - 1) if holding[i] < most]
        mass, left = sum([portions[i] for i in movable]), rest
        for i in movable:
            addition = min(most - holding[i], max(1, left * portions[i] // mass), rest)
            holding[i] = holding[i] + addition
            rest = rest - addition
    return np.array([most] + holding)


def uneven(stream_key, amount, total, most, lean):
    if amount == 2:
        one = jax.random.randint(stream_key, (), max(1, total - most), min(most, total - 1) + 1)
        return jnp.stack([one, total - one])
    sizes = jnp.asarray(profile(amount, total, most, lean), jnp.int32)
    twos = (amount - 1) // 2
    donor, taker = sizes[1:1 + 2 * twos:2], sizes[2:2 + 2 * twos:2]
    margin = jnp.minimum(donor - 1, most - taker)
    passed = jax.random.randint(jax.random.fold_in(stream_key, 1), (twos,), 0, 1 << 20) % (margin + 1)
    sizes = sizes.at[1:1 + 2 * twos:2].set(donor - passed).at[2:2 + 2 * twos:2].set(taker + passed)
    return sizes[jax.random.permutation(jax.random.fold_in(stream_key, 2), amount)]


def centred(own_key, shape, width, most, pieces=(), kind=jnp.bfloat16):
    result = jax.random.normal(own_key, shape, jnp.float32) * width
    if len(pieces) > 0:
        result = block_levels(own_key, shape, pieces, -0.22, 0.18) * result
    return jnp.clip(result, min=-most, max=most).astype(kind)


def setup_inputs(seed: int = 0) -> dict:
    key_list = jax.random.split(jax.random.key(seed), 13)
    hidden_in = draw_hidden_in(jax.random.fold_in(key_list[12], 71), 0)
    out_grad = centred(key_list[1], (TOKENS, MODEL_WIDTH), 0.05, 0.29882812, ((0, 32),))
    seq_lengths = jax.vmap(lambda own: uneven(own, NSEQ, GROUP_TOKENS, MOST, 2))(jax.random.split(key_list[2], N_DP)).reshape((N_DP, NSEQ)).astype(jnp.int32)
    seq_adapter = touch_ends(jax.random.randint(key_list[3], (N_DP, NSEQ), 0, ADAPTER_COUNT), jax.random.fold_in(key_list[3], 1), 0, ADAPTER_COUNT - 1).astype(jnp.int32)
    query_weight = centred(key_list[4], (MODEL_WIDTH, QW), MODEL_WIDTH ** -0.5, 0.0625, ((1, 4),))
    key_value_weight = centred(key_list[5], (2, MODEL_WIDTH, KW), MODEL_WIDTH ** -0.5, 0.0625, ((2, 4),))
    output_weight = centred(key_list[6], (QW, MODEL_WIDTH), QW ** -0.5, 0.09375, ((0, 4),))
    a_in = centred(key_list[7], (ADAPTER_COUNT, 3 * ADAPTER_RANK, MODEL_WIDTH), MODEL_WIDTH ** -0.5, 0.0625, ((0, 8), (2, 4)))
    b_query = centred(key_list[8], (ADAPTER_COUNT, ADAPTER_RANK, QW), 0.0625, 0.375, ((0, 8), (2, 4)))
    b_key_value = centred(key_list[9], (ADAPTER_COUNT, 2, ADAPTER_RANK, KW), 0.0625, 0.375, ((0, 8), (3, 4)))
    output_down_factor = centred(key_list[10], (ADAPTER_COUNT, ADAPTER_RANK, QW), QW ** -0.5, 0.09375, ((0, 8), (2, 4)))
    output_up_factor = centred(key_list[11], (ADAPTER_COUNT, ADAPTER_RANK, MODEL_WIDTH), 0.0625, 0.375, ((0, 8), (1, 4)))
    return {"hidden_in": hidden_in, "out_grad": out_grad, "seq_lengths": seq_lengths, "seq_adapter": seq_adapter, "query_weight": query_weight, "key_value_weight": key_value_weight, "output_weight": output_weight, "a_in": a_in, "b_query": b_query, "b_key_value": b_key_value, "output_down_factor": output_down_factor, "output_up_factor": output_up_factor}


adapter_scale = 2.0
rope_theta = 500000.0
masked_score = -1.0e30


def contract_trailing_axis(left, right):
    return lax.dot_general(left, right, (((1,), (1,)), ((), ())), preferred_element_type=jnp.float32)


def contract_leading_axis(left, right):
    return lax.dot_general(left, right, (((0,), (0,)), ((), ())), preferred_element_type=jnp.float32)


def token_tables(lengths, adapters, tok_total, adapter_overall_count):
    seq_ends = jnp.cumsum(lengths).astype(jnp.int32)
    seq_starts = seq_ends - lengths
    token_ids = jnp.arange(tok_total, dtype=jnp.int32)
    member = ((token_ids[:, None] >= seq_starts[None, :]) & (token_ids[:, None] < seq_ends[None, :])).astype(jnp.int32)
    seq_index = jnp.sum(member * jnp.arange(lengths.shape[0], dtype=jnp.int32)[None, :], axis=1)
    position = token_ids - jnp.sum(member * seq_starts[None, :], axis=1)
    adapter_of = jnp.sum(member * adapters[None, :], axis=1)
    adapter_hot = adapter_of[:, None] == jnp.arange(adapter_overall_count, dtype=jnp.int32)[None, :]
    allowed = (seq_index[:, None] == seq_index[None, :]) & (token_ids[None, :] <= token_ids[:, None])
    return position, adapter_hot, allowed


def rope_tables(position):
    half_dim = HEAD_SIZE // 2
    inverse = rope_theta ** (-(jnp.arange(half_dim, dtype=jnp.float32) * (2.0 / HEAD_SIZE)))
    angle = position.astype(jnp.float32)[:, None] * inverse[None, :]
    cosine_table = jnp.concatenate([jnp.cos(angle), jnp.cos(angle)], axis=1)
    sine_table = jnp.concatenate([jnp.sin(angle), jnp.sin(angle)], axis=1)
    return cosine_table, sine_table


def apply_rotation(vectors, cosine_table, sine_table):
    half_dim = HEAD_SIZE // 2
    turned = jnp.concatenate([-vectors[..., half_dim:], vectors[..., :half_dim]], axis=-1)
    return vectors * cosine_table[:, None, :] + turned * sine_table[:, None, :]


def choose_rank_rows(onehot_single, product, rank_width):
    shaped = product.reshape(product.shape[0], onehot_single.shape[1], rank_width)
    return jnp.sum(shaped * onehot_single[:, :, None], axis=1)


def expand_from_rank(onehot_halfprec, factors):
    return (onehot_halfprec[:, :, None] * factors[:, None, :]).reshape(factors.shape[0], onehot_halfprec.shape[1] * factors.shape[1])


def attend(queries, rotated_keys, incoming_values, allowed):
    tok_total, head_count, _ = queries.shape
    group_count = rotated_keys.shape[1]
    per_group = head_count // group_count
    grouped = queries.reshape(tok_total, group_count, per_group, HEAD_SIZE).astype(jnp.float32)
    scores = jnp.einsum("tgpe,sge->gpts", grouped, rotated_keys.astype(jnp.float32)) * (HEAD_SIZE ** -0.5)
    scores = jnp.where(allowed[None, None], scores, masked_score)
    peak = jnp.max(scores, axis=-1, keepdims=True)
    expped = jnp.exp(scores - peak)
    probs = expped / jnp.sum(expped, axis=-1, keepdims=True)
    probs_bf = probs.astype(jnp.bfloat16)
    blended_output = jnp.einsum("gpts,sge->tgpe", probs_bf.astype(jnp.float32), incoming_values.astype(jnp.float32))
    return blended_output.reshape(tok_total, head_count * HEAD_SIZE).astype(jnp.bfloat16), probs, probs_bf


def attend_back(queries, rotated_keys, incoming_values, probs, probs_bf, blended_gradient):
    tok_total, head_count, _ = queries.shape
    group_count = rotated_keys.shape[1]
    per_group = head_count // group_count
    incoming_gradient = blended_gradient.reshape(tok_total, group_count, per_group, HEAD_SIZE).astype(jnp.float32)
    grad_probs = jnp.einsum("tgpe,sge->gpts", incoming_gradient, incoming_values.astype(jnp.float32))
    grad_values = jnp.einsum("gpts,tgpe->sge", probs_bf.astype(jnp.float32), incoming_gradient)
    inner = jnp.sum(grad_probs * probs, axis=-1, keepdims=True)
    grad_scores = (probs * (grad_probs - inner) * (HEAD_SIZE ** -0.5)).astype(jnp.bfloat16)
    grouped = queries.reshape(tok_total, group_count, per_group, HEAD_SIZE).astype(jnp.float32)
    grad_queries = jnp.einsum("gpts,sge->tgpe", grad_scores.astype(jnp.float32), rotated_keys.astype(jnp.float32))
    grad_keys = jnp.einsum("gpts,tgpe->sge", grad_scores.astype(jnp.float32), grouped)
    return grad_queries.reshape(tok_total, head_count, HEAD_SIZE), grad_keys, grad_values


def reference(hidden_in, out_grad, seq_lengths, seq_adapter, query_weight, key_value_weight, output_weight, a_in, b_query, b_key_value, output_down_factor, output_up_factor):
    block_list = N_TENSOR
    q_block = QW // block_list
    kv_block = KW // block_list
    width_block = MODEL_WIDTH // block_list
    rank_block = ADAPTER_RANK // block_list
    input_down_flattened = a_in.reshape(ADAPTER_COUNT * 3 * ADAPTER_RANK, MODEL_WIDTH)
    query_up_flattened = b_query.reshape(ADAPTER_COUNT * ADAPTER_RANK, QW)
    key_up_flattened = b_key_value[:, 0].reshape(ADAPTER_COUNT * ADAPTER_RANK, KW)
    value_up_flattened = b_key_value[:, 1].reshape(ADAPTER_COUNT * ADAPTER_RANK, KW)
    output_down_flattened = output_down_factor.reshape(ADAPTER_COUNT * ADAPTER_RANK, QW)
    output_up_flattened = output_up_factor.reshape(ADAPTER_COUNT * ADAPTER_RANK, MODEL_WIDTH)

    def one_group(totals, inputs):
        token_rows, incoming_gradient, lengths, adapters = inputs
        position, adapter_hot, allowed = token_tables(lengths, adapters, GROUP_TOKENS, ADAPTER_COUNT)
        onehot_single = adapter_hot.astype(jnp.float32)
        onehot_halfprec = adapter_hot.astype(jnp.bfloat16)
        cosine_table, sine_table = rope_tables(position)
        input_rank_rows = choose_rank_rows(onehot_single, contract_trailing_axis(token_rows, input_down_flattened), 3 * ADAPTER_RANK).astype(jnp.bfloat16)
        adapter_query_delta = expand_from_rank(onehot_halfprec, input_rank_rows[:, :ADAPTER_RANK])
        adapter_key_delta = expand_from_rank(onehot_halfprec, input_rank_rows[:, ADAPTER_RANK:2 * ADAPTER_RANK])
        adapter_value_delta = expand_from_rank(onehot_halfprec, input_rank_rows[:, 2 * ADAPTER_RANK:])
        query_before_rotation = jnp.dot(token_rows, query_weight, preferred_element_type=jnp.float32) + adapter_scale * jnp.dot(adapter_query_delta, query_up_flattened, preferred_element_type=jnp.float32)
        key_before_rotation = jnp.dot(token_rows, key_value_weight[0], preferred_element_type=jnp.float32) + adapter_scale * jnp.dot(adapter_key_delta, key_up_flattened, preferred_element_type=jnp.float32)
        value_projected = jnp.dot(token_rows, key_value_weight[1], preferred_element_type=jnp.float32) + adapter_scale * jnp.dot(adapter_value_delta, value_up_flattened, preferred_element_type=jnp.float32)
        queries = apply_rotation(query_before_rotation.reshape(GROUP_TOKENS, HQ, HEAD_SIZE), cosine_table, sine_table).astype(jnp.bfloat16)
        rotated_keys = apply_rotation(key_before_rotation.reshape(GROUP_TOKENS, KEY_VALUE_HEADS, HEAD_SIZE), cosine_table, sine_table).astype(jnp.bfloat16)
        incoming_values = value_projected.reshape(GROUP_TOKENS, KEY_VALUE_HEADS, HEAD_SIZE).astype(jnp.bfloat16)
        blended_output, probs, probs_bf = attend(queries, rotated_keys, incoming_values, allowed)
        output_rank_rows = choose_rank_rows(onehot_single, contract_trailing_axis(blended_output, output_down_flattened), ADAPTER_RANK).astype(jnp.bfloat16)
        adapter_output_delta = expand_from_rank(onehot_halfprec, output_rank_rows)
        per_head_terms = jnp.einsum("tnk,nkd->ntd", blended_output.reshape(GROUP_TOKENS, block_list, q_block).astype(jnp.float32), output_weight.reshape(block_list, q_block, MODEL_WIDTH).astype(jnp.float32))
        adjacent_terms = jnp.einsum("gzmy,zmys->mgs", adapter_output_delta.reshape(GROUP_TOKENS, ADAPTER_COUNT, block_list, rank_block).astype(jnp.float32), output_up_factor.reshape(ADAPTER_COUNT, block_list, rank_block, MODEL_WIDTH).astype(jnp.float32))
        output_pieces = lax.optimization_barrier((per_head_terms + adapter_scale * adjacent_terms).astype(jnp.bfloat16)).astype(jnp.float32)
        attn_out = jnp.sum(output_pieces, axis=0).astype(jnp.bfloat16)

        output_rank_gradient = (adapter_scale * choose_rank_rows(onehot_single, contract_trailing_axis(incoming_gradient, output_up_flattened), ADAPTER_RANK)).astype(jnp.bfloat16)
        output_up_gradient_group = adapter_scale * contract_leading_axis(adapter_output_delta, incoming_gradient)
        adapter_output_gradient = expand_from_rank(onehot_halfprec, output_rank_gradient)
        blended_gradient = (contract_trailing_axis(incoming_gradient, output_weight) + jnp.dot(adapter_output_gradient, output_down_flattened, preferred_element_type=jnp.float32)).astype(jnp.bfloat16)
        output_down_gradient_group = contract_leading_axis(adapter_output_gradient, blended_output)
        grad_queries, grad_keys, grad_values = attend_back(queries, rotated_keys, incoming_values, probs, probs_bf, blended_gradient)
        query_gradient_rows = apply_rotation(grad_queries, cosine_table, -sine_table).reshape(GROUP_TOKENS, QW).astype(jnp.bfloat16)
        key_gradient_rows = apply_rotation(grad_keys, cosine_table, -sine_table).reshape(GROUP_TOKENS, KW).astype(jnp.bfloat16)
        value_gradient_rows = grad_values.reshape(GROUP_TOKENS, KW).astype(jnp.bfloat16)
        backward_rank_rows = jnp.concatenate([
            choose_rank_rows(onehot_single, contract_trailing_axis(query_gradient_rows, query_up_flattened), ADAPTER_RANK),
            choose_rank_rows(onehot_single, contract_trailing_axis(key_gradient_rows, key_up_flattened), ADAPTER_RANK),
            choose_rank_rows(onehot_single, contract_trailing_axis(value_gradient_rows, value_up_flattened), ADAPTER_RANK)], axis=1)
        input_rank_gradient = (adapter_scale * backward_rank_rows).astype(jnp.bfloat16)
        query_up_gradient_group = adapter_scale * contract_leading_axis(adapter_query_delta, query_gradient_rows)
        key_up_gradient_group = adapter_scale * contract_leading_axis(adapter_key_delta, key_gradient_rows)
        value_up_gradient_group = adapter_scale * contract_leading_axis(adapter_value_delta, value_gradient_rows)
        adapter_input_gradient = expand_from_rank(onehot_halfprec, input_rank_gradient)
        input_down_gradient_group = contract_leading_axis(adapter_input_gradient, token_rows)
        query_terms = jnp.einsum("tnk,dnk->ntd", query_gradient_rows.reshape(GROUP_TOKENS, block_list, q_block).astype(jnp.float32), query_weight.reshape(MODEL_WIDTH, block_list, q_block).astype(jnp.float32))
        key_terms = jnp.einsum("tnk,dnk->ntd", key_gradient_rows.reshape(GROUP_TOKENS, block_list, kv_block).astype(jnp.float32), key_value_weight[0].reshape(MODEL_WIDTH, block_list, kv_block).astype(jnp.float32))
        value_terms = jnp.einsum("tnk,dnk->ntd", value_gradient_rows.reshape(GROUP_TOKENS, block_list, kv_block).astype(jnp.float32), key_value_weight[1].reshape(MODEL_WIDTH, block_list, kv_block).astype(jnp.float32))
        adjacent_input = jnp.dot(adapter_input_gradient, input_down_flattened, preferred_element_type=jnp.float32).reshape(GROUP_TOKENS, block_list, width_block)
        placed = (jnp.eye(block_list, dtype=jnp.float32)[:, None, :, None] * adjacent_input[None]).reshape(block_list, GROUP_TOKENS, MODEL_WIDTH)
        in_parts = lax.optimization_barrier((((query_terms + key_terms) + value_terms) + placed).astype(jnp.bfloat16)).astype(jnp.float32)
        input_grad = jnp.sum(in_parts, axis=0).astype(jnp.bfloat16)
        new_totals = (
            totals[0] + input_down_gradient_group.reshape(ADAPTER_COUNT, 3 * ADAPTER_RANK, MODEL_WIDTH),
            totals[1] + query_up_gradient_group.reshape(ADAPTER_COUNT, ADAPTER_RANK, QW),
            totals[2] + jnp.stack([key_up_gradient_group.reshape(ADAPTER_COUNT, ADAPTER_RANK, KW), value_up_gradient_group.reshape(ADAPTER_COUNT, ADAPTER_RANK, KW)], axis=1),
            totals[3] + output_down_gradient_group.reshape(ADAPTER_COUNT, ADAPTER_RANK, QW),
            totals[4] + output_up_gradient_group.reshape(ADAPTER_COUNT, ADAPTER_RANK, MODEL_WIDTH))
        return new_totals, (attn_out, input_grad)

    start_totals = (
        jnp.zeros((ADAPTER_COUNT, 3 * ADAPTER_RANK, MODEL_WIDTH), jnp.float32),
        jnp.zeros((ADAPTER_COUNT, ADAPTER_RANK, QW), jnp.float32),
        jnp.zeros((ADAPTER_COUNT, 2, ADAPTER_RANK, KW), jnp.float32),
        jnp.zeros((ADAPTER_COUNT, ADAPTER_RANK, QW), jnp.float32),
        jnp.zeros((ADAPTER_COUNT, ADAPTER_RANK, MODEL_WIDTH), jnp.float32))
    inputs = (hidden_in.reshape(N_DP, GROUP_TOKENS, MODEL_WIDTH), out_grad.reshape(N_DP, GROUP_TOKENS, MODEL_WIDTH), seq_lengths, seq_adapter)
    totals, stacked = lax.scan(one_group, start_totals, inputs)
    return (stacked[0].reshape(TOKENS, MODEL_WIDTH), stacked[1].reshape(TOKENS, MODEL_WIDTH), totals[0], totals[1], totals[2], totals[3], totals[4])
```

```python
import functools

import jax
import jax.numpy as jnp
from jax import lax
from jax.experimental import pallas as pl
from jax.experimental.pallas import tpu as pltpu
from jax.sharding import PartitionSpec as P

HEAD_SIZE = 128


MESH = pl.DeviceIdType.MESH
VMEM_BYTES = 60 * 1024 * 1024
ANY = pl.BlockSpec(memory_space=pl.ANY)
VMEM = pl.BlockSpec(memory_space=pltpu.VMEM)


def remote(src, dst, send_sem, recv_sem, device):
    return pltpu.make_async_remote_copy(
        src_ref=src,
        dst_ref=dst,
        send_sem=send_sem,
        recv_sem=recv_sem,
        device_id=device,
        device_id_type=MESH,
    )


def tensor_peers(n):
    me = lax.axis_index("tensor")
    if n == 4:
        across, up = lax.rem(me, 2), lax.div(me, 2)
        return (me, up * 2 + 1 - across, (1 - up) * 2 + across, (1 - up) * 2 + 1 - across)
    return (me,)


def greet(devices):
    barrier = pltpu.get_barrier_semaphore()
    for device in devices:
        pl.semaphore_signal(barrier, inc=1, device_id=device, device_id_type=MESH)
    pl.semaphore_wait(barrier, len(devices))


def tensor_devices(n):
    if n == 4:
        _, by_x, by_y, _ = tensor_peers(n)
        return [{"tensor": by_x}, {"tensor": by_y}]
    me = lax.axis_index("tensor")
    return [{"tensor": lax.rem(me + k, n)} for k in range(1, n)]


def dp_devices(total):
    me = lax.axis_index("dp")
    pairs = total // 2
    spot, core = lax.div(me, 2), lax.rem(me, 2)
    right = lax.rem(spot + 1, pairs) * 2 + core
    left = lax.rem(spot + pairs - 1, pairs) * 2 + core
    return [{"dp": spot * 2 + 1 - core}, {"dp": right}, {"dp": left}]


def gather_kernel(n, total, nt, nd, *refs):
    take = iter(refs)
    t_in = [next(take) for _ in range(nt)]
    d_in = [next(take) for _ in range(nd)]
    t_out = [next(take) for _ in range(nt)]
    d_out = [next(take) for _ in range(nd)]
    stage = [next(take) for _ in range(nt + nd)]
    load_sem, store_sem, t_send, t_recv, d_send, d_recv, s_send, s_recv = take
    pairs = total // 2
    me_dp = lax.axis_index("dp")
    spot, core = lax.div(me_dp, 2), lax.rem(me_dp, 2)
    sibling = {"dp": spot * 2 + 1 - core}
    right, left = {"dp": (spot + 1) * 2 + core}, {"dp": (spot - 1) * 2 + core}
    peers = tensor_peers(n)
    me = peers[0]

    greet(tensor_devices(n) + dp_devices(total))

    def block(i, offset):
        return d_out[i].at[(spot + offset) * 2 + core]

    def to_side(i, direction, step):
        source = d_in[i] if step == 0 else block(i, -step if direction == 0 else step)
        target = block(i, -step if direction == 0 else step)
        return remote(
            source,
            target,
            d_send.at[i, direction, step],
            d_recv.at[i, direction, step],
            right if direction == 0 else left,
        )

    def to_sibling(i, slot):
        offset = 0 if slot == 0 else (-slot if slot < pairs else slot - pairs + 1)
        source = d_in[i] if slot == 0 else block(i, offset)
        return remote(source, block(i, offset), s_send.at[i, slot], s_recv.at[i, slot], sibling)

    def from_sibling(i, slot):
        offset = 0 if slot == 0 else (-slot if slot < pairs else slot - pairs + 1)
        here = d_out[i].at[(spot + offset) * 2 + 1 - core]
        return remote(here, here, s_send.at[i, slot], s_recv.at[i, slot], sibling)

    def from_side(i, direction, step):
        here = block(i, -step if direction == 0 else step)
        return remote(
            here,
            here,
            d_send.at[i, direction, step - 1],
            d_recv.at[i, direction, step - 1],
            sibling,
        )

    if n == 4:
        _, by_x, by_y, _ = peers
        dev_x, dev_y = {"tensor": by_x}, {"tensor": by_y}

    def halves(ref):
        rows = ref.shape[0] // 2
        return ref.at[pl.ds(0, rows)], ref.at[pl.ds(rows, rows)]

    def t_copy(i, which):
        slot, half, device, source = (
            (me, 0, dev_x, None),
            (me, 1, dev_y, None),
            (me, 1, dev_x, None),
            (me, 0, dev_y, None),
            (by_x, 0, dev_y, 1),
            (by_y, 1, dev_x, 1),
        )[which]
        target = halves(t_out[i].at[slot])[half]
        origin = halves(t_in[i])[half] if source is None else target
        return remote(origin, target, t_send.at[i, which], t_recv.at[i, which], device)

    def t_arrival(i, which):
        slot, half = (
            (by_x, 0),
            (by_y, 1),
            (by_x, 1),
            (by_y, 0),
            (peers[3], 0),
            (peers[3], 1),
        )[which]
        here = halves(t_out[i].at[slot])[half]
        return remote(here, here, t_send.at[i, which], t_recv.at[i, which], dev_x)

    def t_direct(i, k, slot):
        return remote(
            t_in[i],
            t_out[i].at[slot],
            t_send.at[i, k],
            t_recv.at[i, k],
            {"tensor": lax.rem(me + k, n)},
        )

    for i in range(nt):
        for k in range(4) if n == 4 else range(1, n):
            (t_copy(i, k) if n == 4 else t_direct(i, k, me)).start()
    for i in range(nd):
        if pairs > 1:
            pl.when(spot + 1 < pairs)(lambda i=i: to_side(i, 0, 0).start())
            pl.when(spot >= 1)(lambda i=i: to_side(i, 1, 0).start())
    for i in range(nd):
        to_sibling(i, 0).start()
    for i, source in enumerate(t_in + d_in):
        pltpu.make_async_copy(source, stage[i], load_sem.at[i]).start()
    for i, target in enumerate([t.at[me] for t in t_out] + [d.at[me_dp] for d in d_out]):
        pltpu.make_async_copy((t_in + d_in)[i], stage[i], load_sem.at[i]).wait()
        pltpu.make_async_copy(stage[i], target, store_sem.at[i]).start()

    def dp_step(step):
        for i in range(nd):

            @pl.when(spot >= step)
            def _(i=i):
                from_side(i, 0, step).wait_recv()
                if step < pairs - 1:
                    pl.when(spot + 1 < pairs)(lambda: to_side(i, 0, step).start())
                to_sibling(i, step).start()

            @pl.when(spot + step < pairs)
            def _(i=i):
                from_side(i, 1, step).wait_recv()
                if step < pairs - 1:
                    pl.when(spot >= 1)(lambda: to_side(i, 1, step).start())
                to_sibling(i, pairs - 1 + step).start()

    if n == 4:
        for i in range(nt):
            t_arrival(i, 0).wait_recv()
            t_copy(i, 4).start()
            t_arrival(i, 1).wait_recv()
            t_copy(i, 5).start()
    for step in range(1, pairs):
        dp_step(step)
    for i in range(nt):
        if n == 4:
            for which in range(2, 6):
                t_arrival(i, which).wait_recv()
            for which in range(6):
                t_copy(i, which).wait_send()
        else:
            for k in range(1, n):
                t_direct(i, k, lax.rem(me + n - k, n)).wait_recv()
            for k in range(1, n):
                t_direct(i, k, me).wait_send()
    for i in range(nd):
        from_sibling(i, 0).wait_recv()
        to_sibling(i, 0).wait_send()
        for step in range(1, pairs):

            @pl.when(spot >= step)
            def _(i=i, step=step):
                from_sibling(i, step).wait_recv()
                to_sibling(i, step).wait_send()

            @pl.when(spot + step < pairs)
            def _(i=i, step=step):
                from_sibling(i, pairs - 1 + step).wait_recv()
                to_sibling(i, pairs - 1 + step).wait_send()

        for step in range(pairs - 1):
            pl.when((spot >= step) & (spot + 1 < pairs))(
                lambda i=i, step=step: to_side(i, 0, step).wait_send()
            )
            pl.when((spot + step < pairs) & (spot >= 1))(
                lambda i=i, step=step: to_side(i, 1, step).wait_send()
            )
    for i, target in enumerate([t.at[me] for t in t_out] + [d.at[me_dp] for d in d_out]):
        pltpu.make_async_copy(stage[i], target, store_sem.at[i]).wait()


def gather_all(tensor_arrays, dp_arrays, collective_id):
    n, total = lax.axis_size("tensor"), lax.axis_size("dp")
    nt, nd = len(tensor_arrays), len(dp_arrays)
    pairs = total // 2
    every = list(tensor_arrays) + list(dp_arrays)
    lead = [n] * nt + [total] * nd
    dma = pltpu.SemaphoreType.DMA
    outs = pl.pallas_call(
        functools.partial(gather_kernel, n, total, nt, nd),
        out_shape=[
            jax.ShapeDtypeStruct((count,) + a.shape, a.dtype) for count, a in zip(lead, every)
        ],
        in_specs=[ANY] * (nt + nd),
        out_specs=[ANY] * (nt + nd),
        scratch_shapes=[pltpu.VMEM(a.shape, a.dtype) for a in every]
        + [
            dma((nt + nd,)),
            dma((nt + nd,)),
            dma((nt, max(n, 6))),
            dma((nt, max(n, 6))),
            dma((nd, 2, pairs)),
            dma((nd, 2, pairs)),
            dma((nd, 2 * pairs)),
            dma((nd, 2 * pairs)),
        ],
        compiler_params=pltpu.CompilerParams(
            collective_id=collective_id, has_side_effects=True, vmem_limit_bytes=VMEM_BYTES
        ),
        name="gather_all",
    )(*every)
    return [o.reshape((o.shape[0] * o.shape[1],) + o.shape[2:]) for o in outs]


def small_sum_kernel(n, in_ref, out_ref, slots, send_sem, recv_sem):
    me = lax.axis_index("tensor")
    greet([{"tensor": lax.rem(me + k, n)} for k in range(1, n)])

    def copy(k, slot):
        return remote(
            in_ref,
            slots.at[slot],
            send_sem.at[k],
            recv_sem.at[k],
            {"tensor": lax.rem(me + k, n)},
        )

    for k in range(1, n):
        copy(k, me).start()
    slots[me] = in_ref[...]
    for k in range(1, n):
        copy(k, lax.rem(me + n - k, n)).wait_recv()
    added = slots[0]
    for j in range(1, n):
        added = added + slots[j]
    out_ref[...] = added
    for k in range(1, n):
        copy(k, me).wait_send()


def small_sum(values, collective_id):
    n = lax.axis_size("tensor")
    flipped = values.T
    summed = pl.pallas_call(
        functools.partial(small_sum_kernel, n),
        out_shape=jax.ShapeDtypeStruct(flipped.shape, flipped.dtype),
        in_specs=[VMEM],
        out_specs=VMEM,
        scratch_shapes=[
            pltpu.VMEM((n,) + flipped.shape, flipped.dtype),
            pltpu.SemaphoreType.DMA((n,)),
            pltpu.SemaphoreType.DMA((n,)),
        ],
        compiler_params=pltpu.CompilerParams(collective_id=collective_id, has_side_effects=True),
        name="small_sum",
    )(flipped)
    return summed.T


def scatter_kernel(n, total, nt, nd, *refs):
    take = iter(refs)
    t_in = [next(take) for _ in range(nt)]
    d_in = [next(take) for _ in range(nd)]
    t_out = [next(take) for _ in range(nt)]
    d_out = [next(take) for _ in range(nd)]
    t_own = [next(take) for _ in range(nt)]
    t_mid = [next(take) for _ in range(nt)]
    t_got = [next(take) for _ in range(nt)]
    t_end = [next(take) for _ in range(nt)]
    d_own = [next(take) for _ in range(nd)]
    d_sib = [next(take) for _ in range(nd)]
    d_side = [next(take) for _ in range(nd)]
    t_load, d_load, t_send, t_recv, d_send, d_recv, s_send, s_recv = take
    pairs = total // 2
    me_dp = lax.axis_index("dp")
    spot, core = lax.div(me_dp, 2), lax.rem(me_dp, 2)
    sibling = {"dp": spot * 2 + 1 - core}
    right, left = {"dp": (spot + 1) * 2 + core}, {"dp": (spot - 1) * 2 + core}
    peers = tensor_peers(n)
    me = peers[0]
    f32 = jnp.float32

    greet(tensor_devices(n) + dp_devices(total))

    for i in range(nd):
        remote(
            d_in[i].at[:, 1 - core], d_sib[i], s_send.at[i], s_recv.at[i], sibling
        ).start()
    for i in range(nd):
        pltpu.make_async_copy(d_in[i].at[:, core], d_own[i], d_load.at[i]).start()
    if n == 4:
        _, by_x, by_y, across = peers
        dev_x, dev_y = {"tensor": by_x}, {"tensor": by_y}
        width = t_in[0].shape[2] // 2
        cut = (pl.ds(0, width), pl.ds(width, width))

    def t_first(i, side, part):
        slot = across if part == 0 else (by_x, by_y)[side]
        return remote(
            t_in[i].at[slot, :, cut[side]],
            t_got[i].at[side, part],
            t_send.at[i, side * 2 + part],
            t_recv.at[i, side * 2 + part],
            (dev_x, dev_y)[side],
        )

    def t_second(i, side):
        return remote(
            t_mid[i].at[side],
            t_end[i].at[side],
            t_send.at[i, 4 + side],
            t_recv.at[i, 4 + side],
            (dev_y, dev_x)[side],
        )

    def t_loads(i):
        loads = [pltpu.make_async_copy(t_in[i].at[me], t_own[i], t_load.at[i, 0])]
        if n == 4:
            for side, slot in ((0, by_y), (1, by_x)):
                loads.append(
                    pltpu.make_async_copy(
                        t_in[i].at[slot, :, cut[side]], t_mid[i].at[side], t_load.at[i, 1 + side]
                    )
                )
        return loads

    def t_direct(i, k, slot, landing):
        return remote(
            t_in[i].at[slot],
            t_got[i].at[landing],
            t_send.at[i, k],
            t_recv.at[i, k],
            {"tensor": lax.rem(me + k, n)},
        )

    for i in range(nt):
        if n == 4:
            for part in range(2):
                for side in range(2):
                    t_first(i, side, part).start()
        else:
            for k in range(1, n):
                t_direct(i, k, lax.rem(me + k, n), me).start()
        for load in t_loads(i):
            load.start()

    for i in range(nd):
        pltpu.make_async_copy(d_in[i].at[:, core], d_own[i], d_load.at[i]).wait()
        remote(
            d_in[i].at[:, 1 - core], d_sib[i], s_send.at[i], s_recv.at[i], sibling
        ).wait_recv()
        for d in range(pairs):
            d_own[i][d] = (d_own[i][d].astype(f32) + d_sib[i][d].astype(f32)).astype(
                d_own[i].dtype
            )

    def d_copy(i, direction, slot, source):
        return remote(
            source,
            d_side[i].at[direction, slot],
            d_send.at[i, direction, slot],
            d_recv.at[i, direction, slot],
            (right, left)[direction],
        )

    def d_step(j):
        for direction, d in ((0, pairs - 1 - j), (1, j)):
            outer = spot == 0 if direction == 0 else spot == pairs - 1
            inner = (
                (spot > 0) & (spot < d) if direction == 0 else (spot < pairs - 1) & (spot > d)
            )

            @pl.when(outer)
            def _(direction=direction, d=d):
                for i in range(nd):
                    d_copy(i, direction, j, d_own[i].at[d]).start()

            @pl.when(inner)
            def _(direction=direction, d=d):
                for i in range(nd):
                    here = d_side[i].at[direction, j]
                    d_copy(i, direction, j, here).wait_recv()
                    here[...] = (here[...].astype(f32) + d_own[i][d].astype(f32)).astype(
                        here.dtype
                    )
                    d_copy(i, direction, j, here).start()

    def t_forward(i):
        loads = t_loads(i)
        for side in range(2):
            loads[1 + side].wait()
            t_first(i, side, 0).wait_recv()
            t_mid[i][side] = (
                t_mid[i][side].astype(f32) + t_got[i][side, 0].astype(f32)
            ).astype(t_mid[i].dtype)
            t_second(i, side).start()

    for j in range(max(pairs - 1, nt)):
        if j < pairs - 1:
            d_step(j)
        if n == 4 and j < nt:
            t_forward(j)

    for i in range(nt):
        t_loads(i)[0].wait()
        if n == 4:
            for side in range(2):
                t_first(i, side, 1).wait_recv()
                t_second(i, side).wait_recv()
                t_out[i][:, cut[side]] = (
                    t_own[i][:, cut[side]].astype(f32)
                    + t_got[i][side, 1].astype(f32)
                    + t_end[i][side].astype(f32)
                ).astype(t_out[i].dtype)
        else:
            added = t_own[i][...].astype(f32)
            for k in range(1, n):
                source = lax.rem(me + n - k, n)
                t_direct(i, k, me, source).wait_recv()
                added = added + t_got[i][source].astype(f32)
            t_out[i][...] = added.astype(t_out[i].dtype)

    for i in range(nd):
        d_out[i][...] = d_own[i][spot].astype(f32)

        @pl.when(spot > 0)
        def _(i=i):
            slot = pairs - 1 - spot
            here = d_side[i].at[0, slot]
            d_copy(i, 0, slot, here).wait_recv()
            d_out[i][...] = d_out[i][...] + here[...].astype(f32)

        @pl.when(spot < pairs - 1)
        def _(i=i):
            here = d_side[i].at[1, spot]
            d_copy(i, 1, spot, here).wait_recv()
            d_out[i][...] = d_out[i][...] + here[...].astype(f32)

    for i in range(nd):
        remote(
            d_in[i].at[:, 1 - core], d_sib[i], s_send.at[i], s_recv.at[i], sibling
        ).wait_send()
        for j in range(pairs - 1):
            for direction, d in ((0, pairs - 1 - j), (1, j)):
                pl.when(spot < d if direction == 0 else spot > d)(
                    lambda i=i, direction=direction, j=j: d_copy(
                        i, direction, j, d_side[i].at[direction, j]
                    ).wait_send()
                )
    for i in range(nt):
        if n == 4:
            for side in range(2):
                t_first(i, side, 0).wait_send()
                t_first(i, side, 1).wait_send()
                t_second(i, side).wait_send()
        else:
            for k in range(1, n):
                t_direct(i, k, lax.rem(me + k, n), me).wait_send()


def scatter_all(tensor_arrays, dp_arrays, collective_id):
    n, total = lax.axis_size("tensor"), lax.axis_size("dp")
    nt, nd = len(tensor_arrays), len(dp_arrays)
    pairs = total // 2
    shaped_t = [a.reshape(n, a.shape[0] // n, a.shape[1]) for a in tensor_arrays]
    shaped_d = [a.reshape(pairs, 2, a.shape[0] // total, a.shape[1]) for a in dp_arrays]
    dma = pltpu.SemaphoreType.DMA
    own = [pltpu.VMEM(a.shape[1:], a.dtype) for a in shaped_t]
    if n == 4:
        halved = [(a.shape[1], a.shape[2] // 2) for a in shaped_t]
        kind = [a.dtype for a in shaped_t]
        mid = [pltpu.VMEM((2,) + h, k) for h, k in zip(halved, kind)]
        got = [pltpu.VMEM((2, 2) + h, k) for h, k in zip(halved, kind)]
        end = [pltpu.VMEM((2,) + h, k) for h, k in zip(halved, kind)]
    else:
        mid = [pltpu.VMEM((16, 128), a.dtype) for a in shaped_t]
        got = [pltpu.VMEM(a.shape, a.dtype) for a in shaped_t]
        end = [pltpu.VMEM((16, 128), a.dtype) for a in shaped_t]
    outs = pl.pallas_call(
        functools.partial(scatter_kernel, n, total, nt, nd),
        out_shape=[jax.ShapeDtypeStruct(a.shape[1:], a.dtype) for a in shaped_t]
        + [jax.ShapeDtypeStruct(a.shape[2:], jnp.float32) for a in shaped_d],
        in_specs=[ANY] * (nt + nd),
        out_specs=[VMEM] * (nt + nd),
        scratch_shapes=own
        + mid
        + got
        + end
        + [pltpu.VMEM((pairs,) + a.shape[2:], a.dtype) for a in shaped_d]
        + [pltpu.VMEM((pairs,) + a.shape[2:], a.dtype) for a in shaped_d]
        + [pltpu.VMEM((2, max(pairs - 1, 1)) + a.shape[2:], a.dtype) for a in shaped_d]
        + [
            dma((nt, 3)),
            dma((nd,)),
            dma((nt, max(n, 6))),
            dma((nt, max(n, 6))),
            dma((nd, 2, pairs)),
            dma((nd, 2, pairs)),
            dma((nd,)),
            dma((nd,)),
        ],
        compiler_params=pltpu.CompilerParams(
            collective_id=collective_id, has_side_effects=True, vmem_limit_bytes=VMEM_BYTES
        ),
        name="scatter_all",
    )(*shaped_t, *shaped_d)
    return outs


adapter_scale = 2.0
rope_theta = 500000.0
masked_score = -1e30


def contract_trailing_axis(left, right):
    return lax.dot_general(
        left, right, (((1,), (1,)), ((), ())), preferred_element_type=jnp.float32
    )


def contract_leading_axis(left, right):
    return lax.dot_general(
        left, right, (((0,), (0,)), ((), ())), preferred_element_type=jnp.float32
    )


def token_tables(lengths, adapters, tok_total, adapter_overall_count):
    seq_ends = jnp.cumsum(lengths)
    seq_starts = seq_ends - lengths
    token_ids = jnp.arange(tok_total, dtype=jnp.int32)
    member = (
        (token_ids[:, None] >= seq_starts[None, :]) & (token_ids[:, None] < seq_ends[None, :])
    ).astype(jnp.int32)
    seq_index = jnp.sum(member * jnp.arange(lengths.shape[0], dtype=jnp.int32)[None, :], axis=1)
    position = token_ids - jnp.sum(member * seq_starts[None, :], axis=1)
    adapter_of = jnp.sum(member * adapters[None, :], axis=1)
    adapter_hot = adapter_of[:, None] == jnp.arange(adapter_overall_count, dtype=jnp.int32)[None, :]
    allowed = (seq_index[:, None] == seq_index[None, :]) & (
        token_ids[None, :] <= token_ids[:, None]
    )
    return (position, adapter_hot, allowed)


def rope_tables(position):
    half_dim = HEAD_SIZE // 2
    inverse = rope_theta ** (-(jnp.arange(half_dim, dtype=jnp.float32) * (2.0 / HEAD_SIZE)))
    angle = position.astype(jnp.float32)[:, None] * inverse[None, :]
    cosine_table = jnp.concatenate([jnp.cos(angle), jnp.cos(angle)], axis=1)
    sine_table = jnp.concatenate([jnp.sin(angle), jnp.sin(angle)], axis=1)
    return (cosine_table, sine_table)


def apply_rotation(vectors, cosine_table, sine_table):
    half_dim = HEAD_SIZE // 2
    turned = jnp.concatenate([-vectors[..., half_dim:], vectors[..., :half_dim]], axis=-1)
    return vectors * cosine_table[:, None, :] + turned * sine_table[:, None, :]


def choose_rank_rows(onehot_single, product, rank_width):
    shaped = product.reshape(product.shape[0], onehot_single.shape[1], rank_width)
    return jnp.sum(shaped * onehot_single[:, :, None], axis=1)


def expand_from_rank(onehot_halfprec, factors):
    return (onehot_halfprec[:, :, None] * factors[:, None, :]).reshape(
        factors.shape[0], onehot_halfprec.shape[1] * factors.shape[1]
    )


def attend(queries, rotated_keys, incoming_values, allowed):
    tok_total, head_count, _ = queries.shape
    group_count = rotated_keys.shape[1]
    per_group = head_count // group_count
    grouped = queries.reshape(tok_total, group_count, per_group, HEAD_SIZE)
    scores = jnp.einsum(
        "tgpe,sge->gpts", grouped, rotated_keys, preferred_element_type=jnp.float32
    ) * HEAD_SIZE ** (-0.5)
    scores = jnp.where(allowed[None, None], scores, masked_score)
    peak = jnp.max(scores, axis=-1, keepdims=True)
    expped = jnp.exp(scores - peak)
    probs = expped / jnp.sum(expped, axis=-1, keepdims=True)
    probs_bf = probs.astype(jnp.bfloat16)
    blended_output = jnp.einsum(
        "gpts,sge->tgpe", probs_bf, incoming_values, preferred_element_type=jnp.float32
    )
    return (
        blended_output.reshape(tok_total, head_count * HEAD_SIZE).astype(jnp.bfloat16),
        probs,
        probs_bf,
    )


def attend_back(queries, rotated_keys, incoming_values, probs, probs_bf, blended_gradient):
    tok_total, head_count, _ = queries.shape
    group_count = rotated_keys.shape[1]
    per_group = head_count // group_count
    incoming_gradient = blended_gradient.reshape(tok_total, group_count, per_group, HEAD_SIZE)
    grad_probs = jnp.einsum(
        "tgpe,sge->gpts", incoming_gradient, incoming_values, preferred_element_type=jnp.float32
    )
    grad_values = jnp.einsum(
        "gpts,tgpe->sge", probs_bf, incoming_gradient, preferred_element_type=jnp.float32
    )
    inner = jnp.sum(grad_probs * probs, axis=-1, keepdims=True)
    grad_scores = (probs * (grad_probs - inner) * HEAD_SIZE ** (-0.5)).astype(jnp.bfloat16)
    grouped = queries.reshape(tok_total, group_count, per_group, HEAD_SIZE)
    grad_queries = jnp.einsum(
        "gpts,sge->tgpe", grad_scores, rotated_keys, preferred_element_type=jnp.float32
    )
    grad_keys = jnp.einsum(
        "gpts,tgpe->sge", grad_scores, grouped, preferred_element_type=jnp.float32
    )
    return (grad_queries.reshape(tok_total, head_count, HEAD_SIZE), grad_keys, grad_values)


def local(
    hidden_in,
    out_grad,
    seq_lengths,
    seq_adapter,
    query_weight,
    key_value_weight,
    output_weight,
    a_in,
    b_query,
    b_key_value,
    output_down_factor,
    output_up_factor,
):
    mesh_parts = lax.axis_size("tensor")
    own_slot = lax.axis_index("tensor")
    tok_rows = hidden_in.shape[0]
    tok_total = tok_rows * mesh_parts
    full_width = hidden_in.shape[1]
    narrow_cast = full_width // mesh_parts
    adapter_rank_rows = output_down_factor.shape[1]
    rank_piece = output_up_factor.shape[1]
    query_columns = query_weight.shape[1]
    key_value_columns = key_value_weight.shape[2]
    (
        gathered,
        input_down_every,
        query_up_every,
        key_value_up_every,
        output_down_every,
        b_out_all,
    ) = gather_all(
        [hidden_in],
        [a_in, b_query, b_key_value, output_down_factor, output_up_factor],
        0,
    )
    out_grad, gathered = lax.optimization_barrier((out_grad, gathered))
    incoming_gradient = lax.all_gather(out_grad, "tensor", axis=0, tiled=True)
    adapter_overall_count = input_down_every.shape[0]
    position, adapter_hot, allowed = token_tables(
        seq_lengths[0], seq_adapter[0], tok_total, adapter_overall_count
    )
    onehot_single = adapter_hot.astype(jnp.float32)
    onehot_halfprec = adapter_hot.astype(jnp.bfloat16)
    cosine_table, sine_table = rope_tables(position)
    input_down_flattened = input_down_every.reshape(
        adapter_overall_count * 3 * adapter_rank_rows, narrow_cast
    )
    query_up_flattened = query_up_every.reshape(
        adapter_overall_count * adapter_rank_rows, query_columns
    )
    key_up_flattened = key_value_up_every[:, 0].reshape(
        adapter_overall_count * adapter_rank_rows, key_value_columns
    )
    value_up_flattened = key_value_up_every[:, 1].reshape(
        adapter_overall_count * adapter_rank_rows, key_value_columns
    )
    output_down_flattened = output_down_every.reshape(
        adapter_overall_count * adapter_rank_rows, query_columns
    )
    output_up_flattened = b_out_all.reshape(adapter_overall_count * rank_piece, full_width)
    col_start = own_slot * narrow_cast
    local_columns = lax.dynamic_slice_in_dim(gathered, col_start, narrow_cast, 1)
    rank_partial_sum = choose_rank_rows(
        onehot_single,
        contract_trailing_axis(local_columns, input_down_flattened),
        3 * adapter_rank_rows,
    )
    input_rank_rows = small_sum(rank_partial_sum, 1).astype(jnp.bfloat16)
    adapter_query_delta = expand_from_rank(onehot_halfprec, input_rank_rows[:, :adapter_rank_rows])
    adapter_key_delta = expand_from_rank(
        onehot_halfprec, input_rank_rows[:, adapter_rank_rows : 2 * adapter_rank_rows]
    )
    adapter_value_delta = expand_from_rank(
        onehot_halfprec, input_rank_rows[:, 2 * adapter_rank_rows :]
    )
    query_before_rotation = jnp.dot(
        gathered, query_weight, preferred_element_type=jnp.float32
    ) + adapter_scale * jnp.dot(
        adapter_query_delta, query_up_flattened, preferred_element_type=jnp.float32
    )
    key_before_rotation = jnp.dot(
        gathered, key_value_weight[0], preferred_element_type=jnp.float32
    ) + adapter_scale * jnp.dot(
        adapter_key_delta, key_up_flattened, preferred_element_type=jnp.float32
    )
    value_projected = jnp.dot(
        gathered, key_value_weight[1], preferred_element_type=jnp.float32
    ) + adapter_scale * jnp.dot(
        adapter_value_delta, value_up_flattened, preferred_element_type=jnp.float32
    )
    queries = apply_rotation(
        query_before_rotation.reshape(tok_total, query_columns // HEAD_SIZE, HEAD_SIZE),
        cosine_table,
        sine_table,
    ).astype(jnp.bfloat16)
    rotated_keys = apply_rotation(
        key_before_rotation.reshape(tok_total, key_value_columns // HEAD_SIZE, HEAD_SIZE),
        cosine_table,
        sine_table,
    ).astype(jnp.bfloat16)
    incoming_values = value_projected.reshape(
        tok_total, key_value_columns // HEAD_SIZE, HEAD_SIZE
    ).astype(jnp.bfloat16)
    blended_output, probs, probs_bf = attend(queries, rotated_keys, incoming_values, allowed)
    output_partial_sum = choose_rank_rows(
        onehot_single,
        contract_trailing_axis(blended_output, output_down_flattened),
        adapter_rank_rows,
    )
    grad_part = (
        adapter_scale
        * choose_rank_rows(
            onehot_single,
            contract_trailing_axis(incoming_gradient, output_up_flattened),
            rank_piece,
        )
    ).astype(jnp.bfloat16)
    placed_part = lax.dynamic_update_slice_in_dim(
        jnp.zeros((tok_total, adapter_rank_rows), jnp.float32),
        grad_part.astype(jnp.float32),
        own_slot * rank_piece,
        1,
    )
    both_ranks = small_sum(jnp.concatenate([output_partial_sum, placed_part], axis=1), 2).astype(
        jnp.bfloat16
    )
    output_rank_rows = both_ranks[:, :adapter_rank_rows]
    output_rank_gradient = both_ranks[:, adapter_rank_rows:]
    adapter_output_delta = expand_from_rank(
        onehot_halfprec,
        lax.dynamic_slice_in_dim(output_rank_rows, own_slot * rank_piece, rank_piece, 1),
    )
    adapter_row_values = adapter_output_delta
    attn_out = lax.psum_scatter(
        (
            jnp.dot(blended_output, output_weight, preferred_element_type=jnp.float32)
            + adapter_scale
            * jnp.dot(adapter_row_values, output_up_flattened, preferred_element_type=jnp.float32)
        ).astype(jnp.bfloat16),
        "tensor",
        scatter_dimension=0,
        tiled=True,
    )
    output_up_gradient = (
        adapter_scale * contract_leading_axis(adapter_output_delta, incoming_gradient)
    ).reshape(adapter_overall_count, rank_piece, full_width)
    adapter_output_gradient = expand_from_rank(onehot_halfprec, output_rank_gradient)
    blended_gradient = (
        contract_trailing_axis(incoming_gradient, output_weight)
        + jnp.dot(
            adapter_output_gradient, output_down_flattened, preferred_element_type=jnp.float32
        )
    ).astype(jnp.bfloat16)
    output_down_gradient = contract_leading_axis(adapter_output_gradient, blended_output).reshape(
        adapter_overall_count, adapter_rank_rows, query_columns
    )
    grad_queries, grad_keys, grad_values = attend_back(
        queries, rotated_keys, incoming_values, probs, probs_bf, blended_gradient
    )
    query_gradient_rows = (
        apply_rotation(grad_queries, cosine_table, -sine_table)
        .reshape(tok_total, query_columns)
        .astype(jnp.bfloat16)
    )
    key_gradient_rows = (
        apply_rotation(grad_keys, cosine_table, -sine_table)
        .reshape(tok_total, key_value_columns)
        .astype(jnp.bfloat16)
    )
    value_gradient_rows = grad_values.reshape(tok_total, key_value_columns).astype(jnp.bfloat16)
    backward_partial_sum = jnp.concatenate(
        [
            choose_rank_rows(
                onehot_single,
                contract_trailing_axis(query_gradient_rows, query_up_flattened),
                adapter_rank_rows,
            ),
            choose_rank_rows(
                onehot_single,
                contract_trailing_axis(key_gradient_rows, key_up_flattened),
                adapter_rank_rows,
            ),
            choose_rank_rows(
                onehot_single,
                contract_trailing_axis(value_gradient_rows, value_up_flattened),
                adapter_rank_rows,
            ),
        ],
        axis=1,
    )
    input_rank_gradient = (adapter_scale * small_sum(backward_partial_sum, 3)).astype(
        jnp.bfloat16
    )
    query_up_gradient = (
        adapter_scale * contract_leading_axis(adapter_query_delta, query_gradient_rows)
    ).reshape(adapter_overall_count, adapter_rank_rows, query_columns)
    key_up_gradient = (
        adapter_scale * contract_leading_axis(adapter_key_delta, key_gradient_rows)
    ).reshape(adapter_overall_count, adapter_rank_rows, key_value_columns)
    value_up_gradient = (
        adapter_scale * contract_leading_axis(adapter_value_delta, value_gradient_rows)
    ).reshape(adapter_overall_count, adapter_rank_rows, key_value_columns)
    grad_b_kv = jnp.stack([key_up_gradient, value_up_gradient], axis=1)
    adapter_input_gradient = expand_from_rank(onehot_halfprec, input_rank_gradient)
    input_down_gradient = contract_leading_axis(adapter_input_gradient, local_columns).reshape(
        adapter_overall_count, 3 * adapter_rank_rows, narrow_cast
    )
    adapter_row_values = adapter_input_gradient
    heads_sum = contract_trailing_axis(query_gradient_rows, query_weight) + contract_trailing_axis(
        key_gradient_rows, key_value_weight[0]
    )
    heads_sum = heads_sum + contract_trailing_axis(value_gradient_rows, key_value_weight[1])
    adjacent_columns = jnp.dot(
        adapter_row_values, input_down_flattened, preferred_element_type=jnp.float32
    )
    placed = lax.dynamic_update_slice_in_dim(
        jnp.zeros((lax.axis_size("tensor") * tok_rows, full_width), jnp.float32),
        adjacent_columns,
        col_start,
        1,
    )
    half = jnp.bfloat16
    wide = lambda grad: grad.reshape(-1, grad.shape[-1]).astype(half)
    input_grad, *summed = scatter_all(
        [(heads_sum + placed).astype(half)],
        [
            wide(input_down_gradient),
            wide(query_up_gradient),
            wide(grad_b_kv),
            wide(output_down_gradient),
            wide(output_up_gradient),
        ],
        4,
    )
    summed_a_in, summed_b_query, summed_b_kv, summed_a_out, summed_b_out = [
        s.reshape(factor.shape)
        for s, factor in zip(
            summed, (a_in, b_query, b_key_value, output_down_factor, output_up_factor)
        )
    ]
    return (
        attn_out,
        input_grad,
        summed_a_in,
        summed_b_query,
        summed_b_kv,
        summed_a_out,
        summed_b_out,
    )


def solution(mesh):
    in_specs = (
        P(("dp", "tensor"), None),
        P(("dp", "tensor"), None),
        P("dp", None),
        P("dp", None),
        P(None, "tensor"),
        P(None, None, "tensor"),
        P("tensor", None),
        P("dp", None, "tensor"),
        P("dp", None, "tensor"),
        P("dp", None, None, "tensor"),
        P("dp", None, "tensor"),
        P("dp", "tensor", None),
    )
    out_specs = (
        P(("dp", "tensor"), None),
        P(("dp", "tensor"), None),
        P("dp", None, "tensor"),
        P("dp", None, "tensor"),
        P("dp", None, None, "tensor"),
        P("dp", None, "tensor"),
        P("dp", "tensor", None),
    )
    return jax.shard_map(local, mesh=mesh, in_specs=in_specs, out_specs=out_specs, check_vma=False)
```

```python
import functools

import jax
import jax.numpy as jnp
from jax import lax
from jax.experimental import pallas as pl
from jax.experimental.pallas import tpu as pltpu
from jax.sharding import PartitionSpec as P

HEAD_SIZE = 128


MESH = pl.DeviceIdType.MESH
VMEM_BYTES = 60 * 1024 * 1024
ANY = pl.BlockSpec(memory_space=pl.ANY)
VMEM = pl.BlockSpec(memory_space=pltpu.VMEM)


def remote(src, dst, send_sem, recv_sem, device):
    return pltpu.make_async_remote_copy(
        src_ref=src,
        dst_ref=dst,
        send_sem=send_sem,
        recv_sem=recv_sem,
        device_id=device,
        device_id_type=MESH,
    )


def tensor_peers(n):
    me = lax.axis_index("tensor")
    if n == 4:
        across, up = lax.rem(me, 2), lax.div(me, 2)
        return (me, up * 2 + 1 - across, (1 - up) * 2 + across, (1 - up) * 2 + 1 - across)
    return (me,)


def greet(devices):
    barrier = pltpu.get_barrier_semaphore()
    for device in devices:
        pl.semaphore_signal(barrier, inc=1, device_id=device, device_id_type=MESH)
    pl.semaphore_wait(barrier, len(devices))


def tensor_devices(n):
    if n == 4:
        _, by_x, by_y, _ = tensor_peers(n)
        return [{"tensor": by_x}, {"tensor": by_y}]
    me = lax.axis_index("tensor")
    return [{"tensor": lax.rem(me + k, n)} for k in range(1, n)]


def dp_devices(total):
    me = lax.axis_index("dp")
    pairs = total // 2
    spot, core = lax.div(me, 2), lax.rem(me, 2)
    right = lax.rem(spot + 1, pairs) * 2 + core
    left = lax.rem(spot + pairs - 1, pairs) * 2 + core
    return [{"dp": spot * 2 + 1 - core}, {"dp": right}, {"dp": left}]


def gather_kernel(n, total, nt, nd, *refs):
    take = iter(refs)
    t_in = [next(take) for _ in range(nt)]
    d_in = [next(take) for _ in range(nd)]
    t_out = [next(take) for _ in range(nt)]
    d_out = [next(take) for _ in range(nd)]
    stage = [next(take) for _ in range(nt + nd)]
    load_sem, store_sem, t_send, t_recv, d_send, d_recv, s_send, s_recv = take
    pairs = total // 2
    me_dp = lax.axis_index("dp")
    spot, core = lax.div(me_dp, 2), lax.rem(me_dp, 2)
    sibling = {"dp": spot * 2 + 1 - core}
    right, left = {"dp": (spot + 1) * 2 + core}, {"dp": (spot - 1) * 2 + core}
    peers = tensor_peers(n)
    me = peers[0]

    greet(tensor_devices(n) + dp_devices(total))

    def block(i, offset):
        return d_out[i].at[(spot + offset) * 2 + core]

    def to_side(i, direction, step):
        source = d_in[i] if step == 0 else block(i, -step if direction == 0 else step)
        target = block(i, -step if direction == 0 else step)
        return remote(
            source,
            target,
            d_send.at[i, direction, step],
            d_recv.at[i, direction, step],
            right if direction == 0 else left,
        )

    def to_sibling(i, slot):
        offset = 0 if slot == 0 else (-slot if slot < pairs else slot - pairs + 1)
        source = d_in[i] if slot == 0 else block(i, offset)
        return remote(source, block(i, offset), s_send.at[i, slot], s_recv.at[i, slot], sibling)

    def from_sibling(i, slot):
        offset = 0 if slot == 0 else (-slot if slot < pairs else slot - pairs + 1)
        here = d_out[i].at[(spot + offset) * 2 + 1 - core]
        return remote(here, here, s_send.at[i, slot], s_recv.at[i, slot], sibling)

    def from_side(i, direction, step):
        here = block(i, -step if direction == 0 else step)
        return remote(
            here,
            here,
            d_send.at[i, direction, step - 1],
            d_recv.at[i, direction, step - 1],
            sibling,
        )

    if n == 4:
        _, by_x, by_y, _ = peers
        dev_x, dev_y = {"tensor": by_x}, {"tensor": by_y}

    def halves(ref):
        rows = ref.shape[0] // 2
        return ref.at[pl.ds(0, rows)], ref.at[pl.ds(rows, rows)]

    def t_copy(i, which):
        slot, half, device, source = (
            (me, 0, dev_x, None),
            (me, 1, dev_y, None),
            (me, 1, dev_x, None),
            (me, 0, dev_y, None),
            (by_x, 0, dev_y, 1),
            (by_y, 1, dev_x, 1),
        )[which]
        target = halves(t_out[i].at[slot])[half]
        origin = halves(t_in[i])[half] if source is None else target
        return remote(origin, target, t_send.at[i, which], t_recv.at[i, which], device)

    def t_arrival(i, which):
        slot, half = (
            (by_x, 0),
            (by_y, 1),
            (by_x, 1),
            (by_y, 0),
            (peers[3], 0),
            (peers[3], 1),
        )[which]
        here = halves(t_out[i].at[slot])[half]
        return remote(here, here, t_send.at[i, which], t_recv.at[i, which], dev_x)

    def t_direct(i, k, slot):
        return remote(
            t_in[i],
            t_out[i].at[slot],
            t_send.at[i, k],
            t_recv.at[i, k],
            {"tensor": lax.rem(me + k, n)},
        )

    for i in range(nt):
        for k in range(4) if n == 4 else range(1, n):
            (t_copy(i, k) if n == 4 else t_direct(i, k, me)).start()
    for i in range(nd):
        if pairs > 1:
            pl.when(spot + 1 < pairs)(lambda i=i: to_side(i, 0, 0).start())
            pl.when(spot >= 1)(lambda i=i: to_side(i, 1, 0).start())
    for i in range(nd):
        to_sibling(i, 0).start()
    for i, source in enumerate(t_in + d_in):
        pltpu.make_async_copy(source, stage[i], load_sem.at[i]).start()
    for i, target in enumerate([t.at[me] for t in t_out] + [d.at[me_dp] for d in d_out]):
        pltpu.make_async_copy((t_in + d_in)[i], stage[i], load_sem.at[i]).wait()
        pltpu.make_async_copy(stage[i], target, store_sem.at[i]).start()

    def dp_step(step):
        for i in range(nd):

            @pl.when(spot >= step)
            def _(i=i):
                from_side(i, 0, step).wait_recv()
                if step < pairs - 1:
                    pl.when(spot + 1 < pairs)(lambda: to_side(i, 0, step).start())
                to_sibling(i, step).start()

            @pl.when(spot + step < pairs)
            def _(i=i):
                from_side(i, 1, step).wait_recv()
                if step < pairs - 1:
                    pl.when(spot >= 1)(lambda: to_side(i, 1, step).start())
                to_sibling(i, pairs - 1 + step).start()

    if n == 4:
        for i in range(nt):
            t_arrival(i, 0).wait_recv()
            t_copy(i, 4).start()
            t_arrival(i, 1).wait_recv()
            t_copy(i, 5).start()
    for step in range(1, pairs):
        dp_step(step)
    for i in range(nt):
        if n == 4:
            for which in range(2, 6):
                t_arrival(i, which).wait_recv()
            for which in range(6):
                t_copy(i, which).wait_send()
        else:
            for k in range(1, n):
                t_direct(i, k, lax.rem(me + n - k, n)).wait_recv()
            for k in range(1, n):
                t_direct(i, k, me).wait_send()
    for i in range(nd):
        from_sibling(i, 0).wait_recv()
        to_sibling(i, 0).wait_send()
        for step in range(1, pairs):

            @pl.when(spot >= step)
            def _(i=i, step=step):
                from_sibling(i, step).wait_recv()
                to_sibling(i, step).wait_send()

            @pl.when(spot + step < pairs)
            def _(i=i, step=step):
                from_sibling(i, pairs - 1 + step).wait_recv()
                to_sibling(i, pairs - 1 + step).wait_send()

        for step in range(pairs - 1):
            pl.when((spot >= step) & (spot + 1 < pairs))(
                lambda i=i, step=step: to_side(i, 0, step).wait_send()
            )
            pl.when((spot + step < pairs) & (spot >= 1))(
                lambda i=i, step=step: to_side(i, 1, step).wait_send()
            )
    for i, target in enumerate([t.at[me] for t in t_out] + [d.at[me_dp] for d in d_out]):
        pltpu.make_async_copy(stage[i], target, store_sem.at[i]).wait()


def gather_all(tensor_arrays, dp_arrays, collective_id):
    n, total = lax.axis_size("tensor"), lax.axis_size("dp")
    nt, nd = len(tensor_arrays), len(dp_arrays)
    pairs = total // 2
    every = list(tensor_arrays) + list(dp_arrays)
    lead = [n] * nt + [total] * nd
    dma = pltpu.SemaphoreType.DMA
    outs = pl.pallas_call(
        functools.partial(gather_kernel, n, total, nt, nd),
        out_shape=[
            jax.ShapeDtypeStruct((count,) + a.shape, a.dtype) for count, a in zip(lead, every)
        ],
        in_specs=[ANY] * (nt + nd),
        out_specs=[ANY] * (nt + nd),
        scratch_shapes=[pltpu.VMEM(a.shape, a.dtype) for a in every]
        + [
            dma((nt + nd,)),
            dma((nt + nd,)),
            dma((nt, max(n, 6))),
            dma((nt, max(n, 6))),
            dma((nd, 2, pairs)),
            dma((nd, 2, pairs)),
            dma((nd, 2 * pairs)),
            dma((nd, 2 * pairs)),
        ],
        compiler_params=pltpu.CompilerParams(
            collective_id=collective_id, has_side_effects=True, vmem_limit_bytes=VMEM_BYTES
        ),
        name="gather_all",
    )(*every)
    return [o.reshape((o.shape[0] * o.shape[1],) + o.shape[2:]) for o in outs]


def small_sum_kernel(n, in_ref, out_ref, slots, send_sem, recv_sem):
    me = lax.axis_index("tensor")
    greet([{"tensor": lax.rem(me + k, n)} for k in range(1, n)])

    def copy(k, slot):
        return remote(
            in_ref,
            slots.at[slot],
            send_sem.at[k],
            recv_sem.at[k],
            {"tensor": lax.rem(me + k, n)},
        )

    for k in range(1, n):
        copy(k, me).start()
    slots[me] = in_ref[...]
    for k in range(1, n):
        copy(k, lax.rem(me + n - k, n)).wait_recv()
    added = slots[0]
    for j in range(1, n):
        added = added + slots[j]
    out_ref[...] = added
    for k in range(1, n):
        copy(k, me).wait_send()


def small_sum(values, collective_id):
    n = lax.axis_size("tensor")
    flipped = values.T
    summed = pl.pallas_call(
        functools.partial(small_sum_kernel, n),
        out_shape=jax.ShapeDtypeStruct(flipped.shape, flipped.dtype),
        in_specs=[VMEM],
        out_specs=VMEM,
        scratch_shapes=[
            pltpu.VMEM((n,) + flipped.shape, flipped.dtype),
            pltpu.SemaphoreType.DMA((n,)),
            pltpu.SemaphoreType.DMA((n,)),
        ],
        compiler_params=pltpu.CompilerParams(collective_id=collective_id, has_side_effects=True),
        name="small_sum",
    )(flipped)
    return summed.T


def finish_kernel(n, total, tile, nd, *refs):
    take = iter(refs)
    rows_ref, adapter_ref, down_ref, query_w, key_value_w = [next(take) for _ in range(5)]
    d_in = [next(take) for _ in range(nd)]
    t_out = next(take)
    d_out = [next(take) for _ in range(nd)]
    part, added, got, end, query_buf, key_value_buf = [next(take) for _ in range(6)]
    d_own = [next(take) for _ in range(nd)]
    d_sib = [next(take) for _ in range(nd)]
    d_side = [next(take) for _ in range(nd)]
    w_sem, d_load, t_send, t_recv, d_send, d_recv, s_send, s_recv = take
    pairs = total // 2
    me_dp = lax.axis_index("dp")
    spot, core = lax.div(me_dp, 2), lax.rem(me_dp, 2)
    sibling = {"dp": spot * 2 + 1 - core}
    right, left = {"dp": (spot + 1) * 2 + core}, {"dp": (spot - 1) * 2 + core}
    peers = tensor_peers(n)
    me = peers[0]
    f32 = jnp.float32
    rows, width = t_out.shape
    half = width // 2
    block = width // n
    steps = half // tile
    query_columns = query_w.shape[1]
    key_value_columns = key_value_w.shape[2]
    if n == 4:
        _, by_x, by_y, across = peers
        dev_x, dev_y = {"tensor": by_x}, {"tensor": by_y}

    def column(step, side):
        return pl.multiple_of(side * half + step * tile, tile)

    def loads(step, side):
        span = pl.ds(column(step, side), tile)
        return (
            pltpu.make_async_copy(query_w.at[span, :], query_buf.at[side], w_sem.at[side, 0]),
            pltpu.make_async_copy(
                key_value_w.at[:, span, :], key_value_buf.at[side], w_sem.at[side, 1]
            ),
        )

    for side in range(2):
        for load in loads(0, side):
            load.start()

    greet(tensor_devices(n) + dp_devices(total))

    def d_pair(i):
        return remote(d_in[i].at[:, 1 - core], d_sib[i], s_send.at[i], s_recv.at[i], sibling)

    for i in range(nd):
        d_pair(i).start()
    for i in range(nd):
        pltpu.make_async_copy(d_in[i].at[:, core], d_own[i], d_load.at[i]).start()

    def span_of(slot):
        return pl.ds(pl.multiple_of(slot * rows, rows), rows)

    def t_first(step, side, which):
        slot = across if which == 0 else (by_x, by_y)[side]
        return remote(
            part.at[span_of(slot), pl.ds(column(step, side), tile)],
            got.at[side, which, :, pl.ds(pl.multiple_of(step * tile, tile), tile)],
            t_send.at[side * 2 + which, step],
            t_recv.at[side * 2 + which, step],
            (dev_x, dev_y)[side],
        )

    def t_second(step, side):
        span = pl.ds(pl.multiple_of(step * tile, tile), tile)
        return remote(
            got.at[side, 0, :, span],
            end.at[side, :, span],
            t_send.at[4 + side, step],
            t_recv.at[4 + side, step],
            (dev_y, dev_x)[side],
        )

    def t_direct(step, side, k, slot, landing):
        span = pl.ds(column(step, side), tile)
        return remote(
            part.at[span_of(slot), span],
            got.at[landing, :, span],
            t_send.at[side * n + k, step],
            t_recv.at[side * n + k, step],
            {"tensor": lax.rem(me + k, n)},
        )

    def compute(step, side):
        for load in loads(step, side):
            load.wait()
        first = column(step, side)
        added[...] = (
            contract_trailing_axis(rows_ref[:, :query_columns], query_buf[side])
            + contract_trailing_axis(
                rows_ref[:, query_columns : query_columns + key_value_columns],
                key_value_buf[side, 0],
            )
            + contract_trailing_axis(
                rows_ref[:, query_columns + key_value_columns :], key_value_buf[side, 1]
            )
        )

        @pl.when(lax.div(first, block) == me)
        def _():
            local_column = pl.multiple_of(first - me * block, tile)
            added[...] += jnp.dot(
                adapter_ref[...],
                down_ref[:, pl.ds(local_column, tile)],
                preferred_element_type=f32,
            )

        part[:, pl.ds(first, tile)] = added[...].astype(part.dtype)

        @pl.when(step + 1 < steps)
        def _():
            for load in loads(step + 1, side):
                load.start()

    def send(step, side):
        if n == 4:
            t_first(step, side, 0).start()
            t_first(step, side, 1).start()
        else:
            for k in range(1, n):
                t_direct(step, side, k, lax.rem(me + k, n), me).start()

    for i in range(nd):
        pltpu.make_async_copy(d_in[i].at[:, core], d_own[i], d_load.at[i]).wait()
        d_pair(i).wait_recv()
        for d in range(pairs):
            d_own[i][d] = (d_own[i][d].astype(f32) + d_sib[i][d].astype(f32)).astype(
                d_own[i].dtype
            )

    def d_copy(i, direction, slot, source):
        return remote(
            source,
            d_side[i].at[direction, slot],
            d_send.at[i, direction, slot],
            d_recv.at[i, direction, slot],
            (right, left)[direction],
        )

    def d_outer(j):
        for direction, d in ((0, pairs - 1 - j), (1, j)):

            @pl.when(spot == 0 if direction == 0 else spot == pairs - 1)
            def _(direction=direction, d=d):
                for i in range(nd):
                    d_copy(i, direction, j, d_own[i].at[d]).start()

    def d_inner(j):
        for direction, d in ((0, pairs - 1 - j), (1, j)):

            @pl.when(
                (spot > 0) & (spot < d) if direction == 0 else (spot < pairs - 1) & (spot > d)
            )
            def _(direction=direction, d=d):
                for i in range(nd):
                    here = d_side[i].at[direction, j]
                    d_copy(i, direction, j, here).wait_recv()
                    here[...] = (here[...].astype(f32) + d_own[i][d].astype(f32)).astype(
                        here.dtype
                    )
                    d_copy(i, direction, j, here).start()

    for j in range(pairs - 1):
        d_outer(j)

    def make(step, carry):
        compute(step, 0)
        pl.when(step > 0)(lambda: send(step - 1, 1))
        compute(step, 1)
        send(step, 0)
        return carry

    lax.fori_loop(0, steps, make, 0)
    send(steps - 1, 1)

    def forward(step, carry):
        for side in range(2):
            slot = (by_y, by_x)[side]
            span = pl.ds(pl.multiple_of(step * tile, tile), tile)
            t_first(step, side, 0).wait_recv()
            got[side, 0, :, span] = (
                got[side, 0, :, span].astype(f32)
                + part[span_of(slot), pl.ds(column(step, side), tile)].astype(f32)
            ).astype(got.dtype)
            t_second(step, side).start()
        return carry

    if pairs > 1:
        d_inner(0)
    if n == 4:
        lax.fori_loop(0, steps, forward, 0)
    for j in range(1, pairs - 1):
        d_inner(j)

    def close(step, carry):
        for side in range(2):
            here = pl.ds(column(step, side), tile)
            total_part = part[span_of(me), here].astype(f32)
            if n == 4:
                span = pl.ds(pl.multiple_of(step * tile, tile), tile)
                t_first(step, side, 1).wait_recv()
                t_second(step, side).wait_recv()
                total_part = total_part + got[side, 1, :, span].astype(f32)
                total_part = total_part + end[side, :, span].astype(f32)
                t_first(step, side, 0).wait_send()
                t_first(step, side, 1).wait_send()
                t_second(step, side).wait_send()
            else:
                for k in range(1, n):
                    source = lax.rem(me + n - k, n)
                    t_direct(step, side, k, me, source).wait_recv()
                    total_part = total_part + got[source, :, here].astype(f32)
                for k in range(1, n):
                    t_direct(step, side, k, lax.rem(me + k, n), me).wait_send()
            t_out[:, here] = total_part.astype(t_out.dtype)
        return carry

    lax.fori_loop(0, steps, close, 0)

    for i in range(nd):
        d_out[i][...] = d_own[i][spot].astype(f32)

        @pl.when(spot > 0)
        def _(i=i):
            slot = pairs - 1 - spot
            here = d_side[i].at[0, slot]
            d_copy(i, 0, slot, here).wait_recv()
            d_out[i][...] = d_out[i][...] + here[...].astype(f32)

        @pl.when(spot < pairs - 1)
        def _(i=i):
            here = d_side[i].at[1, spot]
            d_copy(i, 1, spot, here).wait_recv()
            d_out[i][...] = d_out[i][...] + here[...].astype(f32)

    for i in range(nd):
        d_pair(i).wait_send()
        for j in range(pairs - 1):
            for direction, d in ((0, pairs - 1 - j), (1, j)):
                pl.when(spot < d if direction == 0 else spot > d)(
                    lambda i=i, direction=direction, j=j: d_copy(
                        i, direction, j, d_side[i].at[direction, j]
                    ).wait_send()
                )


def finish_all(gradient_rows, adapter_rows, down, query_w, key_value_w, dp_arrays, collective_id):
    n, total = lax.axis_size("tensor"), lax.axis_size("dp")
    nd = len(dp_arrays)
    pairs = total // 2
    tokens, width = gradient_rows.shape[0], query_w.shape[0]
    rows, half = tokens // n, width // 2
    tile = min(512, half, width // n)
    steps = half // tile
    shaped = [a.reshape(pairs, 2, a.shape[0] // total, a.shape[1]) for a in dp_arrays]
    dma = pltpu.SemaphoreType.DMA
    kind = gradient_rows.dtype
    if n == 4:
        landing = [pltpu.VMEM((2, 2, rows, half), kind), pltpu.VMEM((2, rows, half), kind)]
        flows = 6
    else:
        landing = [pltpu.VMEM((n, rows, width), kind), pltpu.VMEM((16, 128), kind)]
        flows = 2 * n
    return pl.pallas_call(
        functools.partial(finish_kernel, n, total, tile, nd),
        out_shape=[jax.ShapeDtypeStruct((rows, width), kind)]
        + [jax.ShapeDtypeStruct(a.shape[2:], jnp.float32) for a in shaped],
        in_specs=[VMEM] * 3 + [ANY] * (2 + nd),
        out_specs=[VMEM] * (1 + nd),
        scratch_shapes=[
            pltpu.VMEM((tokens, width), kind),
            pltpu.VMEM((tokens, tile), jnp.float32),
            *landing,
            pltpu.VMEM((2, tile, query_w.shape[1]), kind),
            pltpu.VMEM((2, 2, tile, key_value_w.shape[2]), kind),
        ]
        + [pltpu.VMEM((pairs,) + a.shape[2:], a.dtype) for a in shaped]
        + [pltpu.VMEM((pairs,) + a.shape[2:], a.dtype) for a in shaped]
        + [pltpu.VMEM((2, max(pairs - 1, 1)) + a.shape[2:], a.dtype) for a in shaped]
        + [
            dma((2, 2)),
            dma((nd,)),
            dma((flows, steps)),
            dma((flows, steps)),
            dma((nd, 2, pairs)),
            dma((nd, 2, pairs)),
            dma((nd,)),
            dma((nd,)),
        ],
        compiler_params=pltpu.CompilerParams(
            collective_id=collective_id, has_side_effects=True, vmem_limit_bytes=VMEM_BYTES
        ),
        name="finish_all",
    )(gradient_rows, adapter_rows, down, query_w, key_value_w, *shaped)


adapter_scale = 2.0
rope_theta = 500000.0
masked_score = -1e30


def contract_trailing_axis(left, right):
    return lax.dot_general(
        left, right, (((1,), (1,)), ((), ())), preferred_element_type=jnp.float32
    )


def contract_leading_axis(left, right):
    return lax.dot_general(
        left, right, (((0,), (0,)), ((), ())), preferred_element_type=jnp.float32
    )


def token_tables(lengths, adapters, tok_total, adapter_overall_count):
    seq_ends = jnp.cumsum(lengths)
    seq_starts = seq_ends - lengths
    token_ids = jnp.arange(tok_total, dtype=jnp.int32)
    member = (
        (token_ids[:, None] >= seq_starts[None, :]) & (token_ids[:, None] < seq_ends[None, :])
    ).astype(jnp.int32)
    seq_index = jnp.sum(member * jnp.arange(lengths.shape[0], dtype=jnp.int32)[None, :], axis=1)
    position = token_ids - jnp.sum(member * seq_starts[None, :], axis=1)
    adapter_of = jnp.sum(member * adapters[None, :], axis=1)
    adapter_hot = adapter_of[:, None] == jnp.arange(adapter_overall_count, dtype=jnp.int32)[None, :]
    allowed = (seq_index[:, None] == seq_index[None, :]) & (
        token_ids[None, :] <= token_ids[:, None]
    )
    return (position, adapter_hot, allowed)


def rope_tables(position):
    half_dim = HEAD_SIZE // 2
    inverse = rope_theta ** (-(jnp.arange(half_dim, dtype=jnp.float32) * (2.0 / HEAD_SIZE)))
    angle = position.astype(jnp.float32)[:, None] * inverse[None, :]
    cosine_table = jnp.concatenate([jnp.cos(angle), jnp.cos(angle)], axis=1)
    sine_table = jnp.concatenate([jnp.sin(angle), jnp.sin(angle)], axis=1)
    return (cosine_table, sine_table)


def apply_rotation(vectors, cosine_table, sine_table):
    half_dim = HEAD_SIZE // 2
    turned = jnp.concatenate([-vectors[..., half_dim:], vectors[..., :half_dim]], axis=-1)
    return vectors * cosine_table[:, None, :] + turned * sine_table[:, None, :]


def choose_rank_rows(onehot_single, product, rank_width):
    shaped = product.reshape(product.shape[0], onehot_single.shape[1], rank_width)
    return jnp.sum(shaped * onehot_single[:, :, None], axis=1)


def expand_from_rank(onehot_halfprec, factors):
    return (onehot_halfprec[:, :, None] * factors[:, None, :]).reshape(
        factors.shape[0], onehot_halfprec.shape[1] * factors.shape[1]
    )


def attend(queries, rotated_keys, incoming_values, allowed):
    tok_total, head_count, _ = queries.shape
    group_count = rotated_keys.shape[1]
    per_group = head_count // group_count
    grouped = queries.reshape(tok_total, group_count, per_group, HEAD_SIZE)
    scores = jnp.einsum(
        "tgpe,sge->gpts", grouped, rotated_keys, preferred_element_type=jnp.float32
    ) * HEAD_SIZE ** (-0.5)
    scores = jnp.where(allowed[None, None], scores, masked_score)
    peak = jnp.max(scores, axis=-1, keepdims=True)
    expped = jnp.exp(scores - peak)
    probs = expped / jnp.sum(expped, axis=-1, keepdims=True)
    probs_bf = probs.astype(jnp.bfloat16)
    blended_output = jnp.einsum(
        "gpts,sge->tgpe", probs_bf, incoming_values, preferred_element_type=jnp.float32
    )
    return (
        blended_output.reshape(tok_total, head_count * HEAD_SIZE).astype(jnp.bfloat16),
        probs,
        probs_bf,
    )


def attend_back(queries, rotated_keys, incoming_values, probs, probs_bf, blended_gradient):
    tok_total, head_count, _ = queries.shape
    group_count = rotated_keys.shape[1]
    per_group = head_count // group_count
    incoming_gradient = blended_gradient.reshape(tok_total, group_count, per_group, HEAD_SIZE)
    grad_probs = jnp.einsum(
        "tgpe,sge->gpts", incoming_gradient, incoming_values, preferred_element_type=jnp.float32
    )
    grad_values = jnp.einsum(
        "gpts,tgpe->sge", probs_bf, incoming_gradient, preferred_element_type=jnp.float32
    )
    inner = jnp.sum(grad_probs * probs, axis=-1, keepdims=True)
    grad_scores = (probs * (grad_probs - inner) * HEAD_SIZE ** (-0.5)).astype(jnp.bfloat16)
    grouped = queries.reshape(tok_total, group_count, per_group, HEAD_SIZE)
    grad_queries = jnp.einsum(
        "gpts,sge->tgpe", grad_scores, rotated_keys, preferred_element_type=jnp.float32
    )
    grad_keys = jnp.einsum(
        "gpts,tgpe->sge", grad_scores, grouped, preferred_element_type=jnp.float32
    )
    return (grad_queries.reshape(tok_total, head_count, HEAD_SIZE), grad_keys, grad_values)


def local(
    hidden_in,
    out_grad,
    seq_lengths,
    seq_adapter,
    query_weight,
    key_value_weight,
    output_weight,
    a_in,
    b_query,
    b_key_value,
    output_down_factor,
    output_up_factor,
):
    mesh_parts = lax.axis_size("tensor")
    own_slot = lax.axis_index("tensor")
    tok_rows = hidden_in.shape[0]
    tok_total = tok_rows * mesh_parts
    full_width = hidden_in.shape[1]
    narrow_cast = full_width // mesh_parts
    adapter_rank_rows = output_down_factor.shape[1]
    rank_piece = output_up_factor.shape[1]
    query_columns = query_weight.shape[1]
    key_value_columns = key_value_weight.shape[2]
    (
        gathered,
        input_down_every,
        query_up_every,
        key_value_up_every,
        output_down_every,
        b_out_all,
    ) = gather_all(
        [hidden_in],
        [a_in, b_query, b_key_value, output_down_factor, output_up_factor],
        0,
    )
    out_grad, gathered = lax.optimization_barrier((out_grad, gathered))
    incoming_gradient = lax.all_gather(out_grad, "tensor", axis=0, tiled=True)
    adapter_overall_count = input_down_every.shape[0]
    position, adapter_hot, allowed = token_tables(
        seq_lengths[0], seq_adapter[0], tok_total, adapter_overall_count
    )
    onehot_single = adapter_hot.astype(jnp.float32)
    onehot_halfprec = adapter_hot.astype(jnp.bfloat16)
    cosine_table, sine_table = rope_tables(position)
    input_down_flattened = input_down_every.reshape(
        adapter_overall_count * 3 * adapter_rank_rows, narrow_cast
    )
    query_up_flattened = query_up_every.reshape(
        adapter_overall_count * adapter_rank_rows, query_columns
    )
    key_up_flattened = key_value_up_every[:, 0].reshape(
        adapter_overall_count * adapter_rank_rows, key_value_columns
    )
    value_up_flattened = key_value_up_every[:, 1].reshape(
        adapter_overall_count * adapter_rank_rows, key_value_columns
    )
    output_down_flattened = output_down_every.reshape(
        adapter_overall_count * adapter_rank_rows, query_columns
    )
    output_up_flattened = b_out_all.reshape(adapter_overall_count * rank_piece, full_width)
    col_start = own_slot * narrow_cast
    local_columns = lax.dynamic_slice_in_dim(gathered, col_start, narrow_cast, 1)
    rank_partial_sum = choose_rank_rows(
        onehot_single,
        contract_trailing_axis(local_columns, input_down_flattened),
        3 * adapter_rank_rows,
    )
    input_rank_rows = small_sum(rank_partial_sum, 1).astype(jnp.bfloat16)
    adapter_query_delta = expand_from_rank(onehot_halfprec, input_rank_rows[:, :adapter_rank_rows])
    adapter_key_delta = expand_from_rank(
        onehot_halfprec, input_rank_rows[:, adapter_rank_rows : 2 * adapter_rank_rows]
    )
    adapter_value_delta = expand_from_rank(
        onehot_halfprec, input_rank_rows[:, 2 * adapter_rank_rows :]
    )
    query_before_rotation = jnp.dot(
        gathered, query_weight, preferred_element_type=jnp.float32
    ) + adapter_scale * jnp.dot(
        adapter_query_delta, query_up_flattened, preferred_element_type=jnp.float32
    )
    key_before_rotation = jnp.dot(
        gathered, key_value_weight[0], preferred_element_type=jnp.float32
    ) + adapter_scale * jnp.dot(
        adapter_key_delta, key_up_flattened, preferred_element_type=jnp.float32
    )
    value_projected = jnp.dot(
        gathered, key_value_weight[1], preferred_element_type=jnp.float32
    ) + adapter_scale * jnp.dot(
        adapter_value_delta, value_up_flattened, preferred_element_type=jnp.float32
    )
    queries = apply_rotation(
        query_before_rotation.reshape(tok_total, query_columns // HEAD_SIZE, HEAD_SIZE),
        cosine_table,
        sine_table,
    ).astype(jnp.bfloat16)
    rotated_keys = apply_rotation(
        key_before_rotation.reshape(tok_total, key_value_columns // HEAD_SIZE, HEAD_SIZE),
        cosine_table,
        sine_table,
    ).astype(jnp.bfloat16)
    incoming_values = value_projected.reshape(
        tok_total, key_value_columns // HEAD_SIZE, HEAD_SIZE
    ).astype(jnp.bfloat16)
    blended_output, probs, probs_bf = attend(queries, rotated_keys, incoming_values, allowed)
    output_partial_sum = choose_rank_rows(
        onehot_single,
        contract_trailing_axis(blended_output, output_down_flattened),
        adapter_rank_rows,
    )
    grad_part = (
        adapter_scale
        * choose_rank_rows(
            onehot_single,
            contract_trailing_axis(incoming_gradient, output_up_flattened),
            rank_piece,
        )
    ).astype(jnp.bfloat16)
    placed_part = lax.dynamic_update_slice_in_dim(
        jnp.zeros((tok_total, adapter_rank_rows), jnp.float32),
        grad_part.astype(jnp.float32),
        own_slot * rank_piece,
        1,
    )
    both_ranks = small_sum(jnp.concatenate([output_partial_sum, placed_part], axis=1), 2).astype(
        jnp.bfloat16
    )
    output_rank_rows = both_ranks[:, :adapter_rank_rows]
    output_rank_gradient = both_ranks[:, adapter_rank_rows:]
    adapter_output_delta = expand_from_rank(
        onehot_halfprec,
        lax.dynamic_slice_in_dim(output_rank_rows, own_slot * rank_piece, rank_piece, 1),
    )
    adapter_row_values = adapter_output_delta
    attn_out = lax.psum_scatter(
        (
            jnp.dot(blended_output, output_weight, preferred_element_type=jnp.float32)
            + adapter_scale
            * jnp.dot(adapter_row_values, output_up_flattened, preferred_element_type=jnp.float32)
        ).astype(jnp.bfloat16),
        "tensor",
        scatter_dimension=0,
        tiled=True,
    )
    output_up_gradient = (
        adapter_scale * contract_leading_axis(adapter_output_delta, incoming_gradient)
    ).reshape(adapter_overall_count, rank_piece, full_width)
    adapter_output_gradient = expand_from_rank(onehot_halfprec, output_rank_gradient)
    blended_gradient = (
        contract_trailing_axis(incoming_gradient, output_weight)
        + jnp.dot(
            adapter_output_gradient, output_down_flattened, preferred_element_type=jnp.float32
        )
    ).astype(jnp.bfloat16)
    output_down_gradient = contract_leading_axis(adapter_output_gradient, blended_output).reshape(
        adapter_overall_count, adapter_rank_rows, query_columns
    )
    grad_queries, grad_keys, grad_values = attend_back(
        queries, rotated_keys, incoming_values, probs, probs_bf, blended_gradient
    )
    query_gradient_rows = (
        apply_rotation(grad_queries, cosine_table, -sine_table)
        .reshape(tok_total, query_columns)
        .astype(jnp.bfloat16)
    )
    key_gradient_rows = (
        apply_rotation(grad_keys, cosine_table, -sine_table)
        .reshape(tok_total, key_value_columns)
        .astype(jnp.bfloat16)
    )
    value_gradient_rows = grad_values.reshape(tok_total, key_value_columns).astype(jnp.bfloat16)
    backward_partial_sum = jnp.concatenate(
        [
            choose_rank_rows(
                onehot_single,
                contract_trailing_axis(query_gradient_rows, query_up_flattened),
                adapter_rank_rows,
            ),
            choose_rank_rows(
                onehot_single,
                contract_trailing_axis(key_gradient_rows, key_up_flattened),
                adapter_rank_rows,
            ),
            choose_rank_rows(
                onehot_single,
                contract_trailing_axis(value_gradient_rows, value_up_flattened),
                adapter_rank_rows,
            ),
        ],
        axis=1,
    )
    input_rank_gradient = (adapter_scale * small_sum(backward_partial_sum, 3)).astype(
        jnp.bfloat16
    )
    query_up_gradient = (
        adapter_scale * contract_leading_axis(adapter_query_delta, query_gradient_rows)
    ).reshape(adapter_overall_count, adapter_rank_rows, query_columns)
    key_up_gradient = (
        adapter_scale * contract_leading_axis(adapter_key_delta, key_gradient_rows)
    ).reshape(adapter_overall_count, adapter_rank_rows, key_value_columns)
    value_up_gradient = (
        adapter_scale * contract_leading_axis(adapter_value_delta, value_gradient_rows)
    ).reshape(adapter_overall_count, adapter_rank_rows, key_value_columns)
    grad_b_kv = jnp.stack([key_up_gradient, value_up_gradient], axis=1)
    adapter_input_gradient = expand_from_rank(onehot_halfprec, input_rank_gradient)
    input_down_gradient = contract_leading_axis(adapter_input_gradient, local_columns).reshape(
        adapter_overall_count, 3 * adapter_rank_rows, narrow_cast
    )
    half = jnp.bfloat16
    wide = lambda grad: grad.reshape(-1, grad.shape[-1]).astype(half)
    input_grad, *summed = finish_all(
        jnp.concatenate([query_gradient_rows, key_gradient_rows, value_gradient_rows], axis=1),
        adapter_input_gradient,
        input_down_flattened,
        query_weight,
        key_value_weight,
        [
            wide(input_down_gradient),
            wide(query_up_gradient),
            wide(grad_b_kv),
            wide(output_down_gradient),
            wide(output_up_gradient),
        ],
        4,
    )
    summed_a_in, summed_b_query, summed_b_kv, summed_a_out, summed_b_out = [
        s.reshape(factor.shape)
        for s, factor in zip(
            summed, (a_in, b_query, b_key_value, output_down_factor, output_up_factor)
        )
    ]
    return (
        attn_out,
        input_grad,
        summed_a_in,
        summed_b_query,
        summed_b_kv,
        summed_a_out,
        summed_b_out,
    )


def solution(mesh):
    in_specs = (
        P(("dp", "tensor"), None),
        P(("dp", "tensor"), None),
        P("dp", None),
        P("dp", None),
        P(None, "tensor"),
        P(None, None, "tensor"),
        P("tensor", None),
        P("dp", None, "tensor"),
        P("dp", None, "tensor"),
        P("dp", None, None, "tensor"),
        P("dp", None, "tensor"),
        P("dp", "tensor", None),
    )
    out_specs = (
        P(("dp", "tensor"), None),
        P(("dp", "tensor"), None),
        P("dp", None, "tensor"),
        P("dp", None, "tensor"),
        P("dp", None, None, "tensor"),
        P("dp", None, "tensor"),
        P("dp", "tensor", None),
    )
    return jax.shard_map(local, mesh=mesh, in_specs=in_specs, out_specs=out_specs, check_vma=False)
```

```python
import functools

import jax
import jax.numpy as jnp
from jax import lax
from jax.experimental import pallas as pl
from jax.experimental.pallas import tpu as pltpu
from jax.sharding import PartitionSpec as P

HEAD_SIZE = 128


MESH = pl.DeviceIdType.MESH
VMEM_BYTES = 60 * 1024 * 1024
ANY = pl.BlockSpec(memory_space=pl.ANY)
VMEM = pl.BlockSpec(memory_space=pltpu.VMEM)


def remote(src, dst, send_sem, recv_sem, device):
    return pltpu.make_async_remote_copy(
        src_ref=src,
        dst_ref=dst,
        send_sem=send_sem,
        recv_sem=recv_sem,
        device_id=device,
        device_id_type=MESH,
    )


def tensor_peers(n):
    me = lax.axis_index("tensor")
    if n == 4:
        across, up = lax.rem(me, 2), lax.div(me, 2)
        return (me, up * 2 + 1 - across, (1 - up) * 2 + across, (1 - up) * 2 + 1 - across)
    return (me,)


def greet(devices):
    barrier = pltpu.get_barrier_semaphore()
    for device in devices:
        pl.semaphore_signal(barrier, inc=1, device_id=device, device_id_type=MESH)
    pl.semaphore_wait(barrier, len(devices))


def tensor_devices(n):
    if n == 4:
        _, by_x, by_y, _ = tensor_peers(n)
        return [{"tensor": by_x}, {"tensor": by_y}]
    me = lax.axis_index("tensor")
    return [{"tensor": lax.rem(me + k, n)} for k in range(1, n)]


def dp_devices(total):
    me = lax.axis_index("dp")
    pairs = total // 2
    spot, core = lax.div(me, 2), lax.rem(me, 2)
    right = lax.rem(spot + 1, pairs) * 2 + core
    left = lax.rem(spot + pairs - 1, pairs) * 2 + core
    return [{"dp": spot * 2 + 1 - core}, {"dp": right}, {"dp": left}]


def gather_kernel(n, total, nt, nd, *refs):
    take = iter(refs)
    t_in = [next(take) for _ in range(nt)]
    d_in = [next(take) for _ in range(nd)]
    query_w, key_value_w = next(take), next(take)
    t_out = [next(take) for _ in range(nt)]
    d_out = [next(take) for _ in range(nd)]
    projected, held, query_buf, key_value_buf, w_sem, h_sem = (next(take) for _ in range(6))
    stage = [next(take) for _ in range(nt + nd)]
    load_sem, store_sem, t_send, t_recv, d_send, d_recv, s_send, s_recv = take
    pairs = total // 2
    me_dp = lax.axis_index("dp")
    spot, core = lax.div(me_dp, 2), lax.rem(me_dp, 2)
    sibling = {"dp": spot * 2 + 1 - core}
    right, left = {"dp": (spot + 1) * 2 + core}, {"dp": (spot - 1) * 2 + core}
    peers = tensor_peers(n)
    me = peers[0]

    rows = t_in[0].shape[0]
    depth = query_buf.shape[1]
    steps = t_in[0].shape[1] // depth
    query_columns = query_w.shape[1]
    key_value_columns = key_value_w.shape[2]

    def loads(step):
        span, slot = pl.ds(pl.multiple_of(step * depth, depth), depth), lax.rem(step, 2)
        return (
            pltpu.make_async_copy(query_w.at[span, :], query_buf.at[slot], w_sem.at[slot, 0]),
            pltpu.make_async_copy(
                key_value_w.at[:, span, :], key_value_buf.at[slot], w_sem.at[slot, 1]
            ),
        )

    def hold(k):
        slot = lax.rem(me + k, n)
        source = t_in[0] if k == 0 else t_out[0].at[slot]
        target = held.at[pl.ds(pl.multiple_of(slot * rows, rows), rows)]
        return pltpu.make_async_copy(source, target, h_sem.at[k])

    def project(step, carry):
        for load in loads(step):
            load.wait()

        @pl.when(step + 1 < steps)
        def _():
            for load in loads(step + 1):
                load.start()

        slot = lax.rem(step, 2)
        chunk = held[:, pl.ds(pl.multiple_of(step * depth, depth), depth)]
        at = query_columns
        for weights, first, width in (
            (query_buf[slot], 0, query_columns),
            (key_value_buf[slot, 0], at, key_value_columns),
            (key_value_buf[slot, 1], at + key_value_columns, key_value_columns),
        ):
            projected[:, first : first + width] += jnp.dot(
                chunk, weights, preferred_element_type=jnp.float32
            )
        return carry

    greet(tensor_devices(n) + dp_devices(total))

    def block(i, offset):
        return d_out[i].at[(spot + offset) * 2 + core]

    def to_side(i, direction, step):
        source = d_in[i] if step == 0 else block(i, -step if direction == 0 else step)
        target = block(i, -step if direction == 0 else step)
        return remote(
            source,
            target,
            d_send.at[i, direction, step],
            d_recv.at[i, direction, step],
            right if direction == 0 else left,
        )

    def to_sibling(i, slot):
        offset = 0 if slot == 0 else (-slot if slot < pairs else slot - pairs + 1)
        source = d_in[i] if slot == 0 else block(i, offset)
        return remote(source, block(i, offset), s_send.at[i, slot], s_recv.at[i, slot], sibling)

    def from_sibling(i, slot):
        offset = 0 if slot == 0 else (-slot if slot < pairs else slot - pairs + 1)
        here = d_out[i].at[(spot + offset) * 2 + 1 - core]
        return remote(here, here, s_send.at[i, slot], s_recv.at[i, slot], sibling)

    def from_side(i, direction, step):
        here = block(i, -step if direction == 0 else step)
        return remote(
            here,
            here,
            d_send.at[i, direction, step - 1],
            d_recv.at[i, direction, step - 1],
            sibling,
        )

    if n == 4:
        _, by_x, by_y, _ = peers
        dev_x, dev_y = {"tensor": by_x}, {"tensor": by_y}

    def halves(ref):
        rows = ref.shape[0] // 2
        return ref.at[pl.ds(0, rows)], ref.at[pl.ds(rows, rows)]

    def t_copy(i, which):
        slot, half, device, source = (
            (me, 0, dev_x, None),
            (me, 1, dev_y, None),
            (me, 1, dev_x, None),
            (me, 0, dev_y, None),
            (by_x, 0, dev_y, 1),
            (by_y, 1, dev_x, 1),
        )[which]
        target = halves(t_out[i].at[slot])[half]
        origin = halves(t_in[i])[half] if source is None else target
        return remote(origin, target, t_send.at[i, which], t_recv.at[i, which], device)

    def t_arrival(i, which):
        slot, half = (
            (by_x, 0),
            (by_y, 1),
            (by_x, 1),
            (by_y, 0),
            (peers[3], 0),
            (peers[3], 1),
        )[which]
        here = halves(t_out[i].at[slot])[half]
        return remote(here, here, t_send.at[i, which], t_recv.at[i, which], dev_x)

    def t_direct(i, k, slot):
        return remote(
            t_in[i],
            t_out[i].at[slot],
            t_send.at[i, k],
            t_recv.at[i, k],
            {"tensor": lax.rem(me + k, n)},
        )

    for i in range(nt):
        for k in range(4) if n == 4 else range(1, n):
            (t_copy(i, k) if n == 4 else t_direct(i, k, me)).start()
    for i in range(nd):
        if pairs > 1:
            pl.when(spot + 1 < pairs)(lambda i=i: to_side(i, 0, 0).start())
            pl.when(spot >= 1)(lambda i=i: to_side(i, 1, 0).start())
    for i in range(nd):
        to_sibling(i, 0).start()
    for i, source in enumerate(t_in + d_in):
        pltpu.make_async_copy(source, stage[i], load_sem.at[i]).start()
    for i, target in enumerate([t.at[me] for t in t_out] + [d.at[me_dp] for d in d_out]):
        pltpu.make_async_copy((t_in + d_in)[i], stage[i], load_sem.at[i]).wait()
        pltpu.make_async_copy(stage[i], target, store_sem.at[i]).start()

    def dp_step(step):
        for i in range(nd):

            @pl.when(spot >= step)
            def _(i=i):
                from_side(i, 0, step).wait_recv()
                if step < pairs - 1:
                    pl.when(spot + 1 < pairs)(lambda: to_side(i, 0, step).start())
                to_sibling(i, step).start()

            @pl.when(spot + step < pairs)
            def _(i=i):
                from_side(i, 1, step).wait_recv()
                if step < pairs - 1:
                    pl.when(spot >= 1)(lambda: to_side(i, 1, step).start())
                to_sibling(i, pairs - 1 + step).start()

    if n == 4:
        for i in range(nt):
            t_arrival(i, 0).wait_recv()
            t_copy(i, 4).start()
            t_arrival(i, 1).wait_recv()
            t_copy(i, 5).start()
    hold(0).start()
    for load in loads(0):
        load.start()
    projected[...] = jnp.zeros_like(projected)
    for step in range(1, max(pairs - 1, 1)):
        dp_step(step)
    for i in range(nt):
        if n == 4:
            for which in range(2, 6):
                t_arrival(i, which).wait_recv()
        else:
            for k in range(1, n):
                t_direct(i, k, lax.rem(me + n - k, n)).wait_recv()
    for k in range(1, n):
        hold(k).start()
    for k in range(n):
        hold(k).wait()
    lax.fori_loop(0, steps, project, 0)
    if pairs > 1:
        dp_step(pairs - 1)
    for i in range(nt):
        if n == 4:
            for which in range(6):
                t_copy(i, which).wait_send()
        else:
            for k in range(1, n):
                t_direct(i, k, me).wait_send()
    for i in range(nd):
        from_sibling(i, 0).wait_recv()
        to_sibling(i, 0).wait_send()
        for step in range(1, pairs):

            @pl.when(spot >= step)
            def _(i=i, step=step):
                from_sibling(i, step).wait_recv()
                to_sibling(i, step).wait_send()

            @pl.when(spot + step < pairs)
            def _(i=i, step=step):
                from_sibling(i, pairs - 1 + step).wait_recv()
                to_sibling(i, pairs - 1 + step).wait_send()

        for step in range(pairs - 1):
            pl.when((spot >= step) & (spot + 1 < pairs))(
                lambda i=i, step=step: to_side(i, 0, step).wait_send()
            )
            pl.when((spot + step < pairs) & (spot >= 1))(
                lambda i=i, step=step: to_side(i, 1, step).wait_send()
            )
    for i, target in enumerate([t.at[me] for t in t_out] + [d.at[me_dp] for d in d_out]):
        pltpu.make_async_copy(stage[i], target, store_sem.at[i]).wait()


def gather_all(tensor_arrays, dp_arrays, query_w, key_value_w, collective_id):
    n, total = lax.axis_size("tensor"), lax.axis_size("dp")
    nt, nd = len(tensor_arrays), len(dp_arrays)
    pairs = total // 2
    every = list(tensor_arrays) + list(dp_arrays)
    lead = [n] * nt + [total] * nd
    dma = pltpu.SemaphoreType.DMA
    tokens, width = tensor_arrays[0].shape[0] * n, tensor_arrays[0].shape[1]
    columns = query_w.shape[1] + 2 * key_value_w.shape[2]
    depth = min(1024, width)
    outs = pl.pallas_call(
        functools.partial(gather_kernel, n, total, nt, nd),
        out_shape=[
            jax.ShapeDtypeStruct((count,) + a.shape, a.dtype) for count, a in zip(lead, every)
        ]
        + [jax.ShapeDtypeStruct((tokens, columns), jnp.float32)],
        in_specs=[ANY] * (nt + nd + 2),
        out_specs=[ANY] * (nt + nd) + [VMEM],
        scratch_shapes=[
            pltpu.VMEM((tokens, width), query_w.dtype),
            pltpu.VMEM((2, depth, query_w.shape[1]), query_w.dtype),
            pltpu.VMEM((2, 2, depth, key_value_w.shape[2]), query_w.dtype),
            dma((2, 2)),
            dma((n,)),
        ]
        + [pltpu.VMEM(a.shape, a.dtype) for a in every]
        + [
            dma((nt + nd,)),
            dma((nt + nd,)),
            dma((nt, max(n, 6))),
            dma((nt, max(n, 6))),
            dma((nd, 2, pairs)),
            dma((nd, 2, pairs)),
            dma((nd, 2 * pairs)),
            dma((nd, 2 * pairs)),
        ],
        compiler_params=pltpu.CompilerParams(
            collective_id=collective_id, has_side_effects=True, vmem_limit_bytes=VMEM_BYTES
        ),
        name="gather_all",
    )(*every, query_w, key_value_w)
    *outs, projected = outs
    return [projected] + [o.reshape((o.shape[0] * o.shape[1],) + o.shape[2:]) for o in outs]


def small_sum_kernel(n, in_ref, out_ref, slots, send_sem, recv_sem):
    me = lax.axis_index("tensor")
    greet([{"tensor": lax.rem(me + k, n)} for k in range(1, n)])

    def copy(k, slot):
        return remote(
            in_ref,
            slots.at[slot],
            send_sem.at[k],
            recv_sem.at[k],
            {"tensor": lax.rem(me + k, n)},
        )

    for k in range(1, n):
        copy(k, me).start()
    slots[me] = in_ref[...]
    for k in range(1, n):
        copy(k, lax.rem(me + n - k, n)).wait_recv()
    added = slots[0]
    for j in range(1, n):
        added = added + slots[j]
    out_ref[...] = added
    for k in range(1, n):
        copy(k, me).wait_send()


def small_sum(values, collective_id):
    n = lax.axis_size("tensor")
    flipped = values.T
    summed = pl.pallas_call(
        functools.partial(small_sum_kernel, n),
        out_shape=jax.ShapeDtypeStruct(flipped.shape, flipped.dtype),
        in_specs=[VMEM],
        out_specs=VMEM,
        scratch_shapes=[
            pltpu.VMEM((n,) + flipped.shape, flipped.dtype),
            pltpu.SemaphoreType.DMA((n,)),
            pltpu.SemaphoreType.DMA((n,)),
        ],
        compiler_params=pltpu.CompilerParams(collective_id=collective_id, has_side_effects=True),
        name="small_sum",
    )(flipped)
    return summed.T


def finish_kernel(n, total, tile, nd, *refs):
    take = iter(refs)
    rows_ref, adapter_ref, down_ref, query_w, key_value_w = [next(take) for _ in range(5)]
    d_in = [next(take) for _ in range(nd)]
    t_out = next(take)
    d_out = [next(take) for _ in range(nd)]
    part, added, got, end, query_buf, key_value_buf = [next(take) for _ in range(6)]
    d_own = [next(take) for _ in range(nd)]
    d_sib = [next(take) for _ in range(nd)]
    d_side = [next(take) for _ in range(nd)]
    w_sem, d_load, t_send, t_recv, d_send, d_recv, s_send, s_recv = take
    pairs = total // 2
    me_dp = lax.axis_index("dp")
    spot, core = lax.div(me_dp, 2), lax.rem(me_dp, 2)
    sibling = {"dp": spot * 2 + 1 - core}
    right, left = {"dp": (spot + 1) * 2 + core}, {"dp": (spot - 1) * 2 + core}
    peers = tensor_peers(n)
    me = peers[0]
    f32 = jnp.float32
    rows, width = t_out.shape
    half = width // 2
    block = width // n
    steps = half // tile
    query_columns = query_w.shape[1]
    key_value_columns = key_value_w.shape[2]
    if n == 4:
        _, by_x, by_y, across = peers
        dev_x, dev_y = {"tensor": by_x}, {"tensor": by_y}

    def column(step, side):
        return pl.multiple_of(side * half + step * tile, tile)

    def loads(step, side):
        span = pl.ds(column(step, side), tile)
        return (
            pltpu.make_async_copy(query_w.at[span, :], query_buf.at[side], w_sem.at[side, 0]),
            pltpu.make_async_copy(
                key_value_w.at[:, span, :], key_value_buf.at[side], w_sem.at[side, 1]
            ),
        )

    for side in range(2):
        for load in loads(0, side):
            load.start()

    greet(tensor_devices(n) + dp_devices(total))

    def d_pair(i):
        return remote(d_in[i].at[:, 1 - core], d_sib[i], s_send.at[i], s_recv.at[i], sibling)

    for i in range(nd):
        d_pair(i).start()
    for i in range(nd):
        pltpu.make_async_copy(d_in[i].at[:, core], d_own[i], d_load.at[i]).start()

    def span_of(slot):
        return pl.ds(pl.multiple_of(slot * rows, rows), rows)

    def t_first(step, side, which):
        slot = across if which == 0 else (by_x, by_y)[side]
        return remote(
            part.at[span_of(slot), pl.ds(column(step, side), tile)],
            got.at[side, which, :, pl.ds(pl.multiple_of(step * tile, tile), tile)],
            t_send.at[side * 2 + which, step],
            t_recv.at[side * 2 + which, step],
            (dev_x, dev_y)[side],
        )

    def t_second(step, side):
        span = pl.ds(pl.multiple_of(step * tile, tile), tile)
        return remote(
            got.at[side, 0, :, span],
            end.at[side, :, span],
            t_send.at[4 + side, step],
            t_recv.at[4 + side, step],
            (dev_y, dev_x)[side],
        )

    def t_direct(step, side, k, slot, landing):
        span = pl.ds(column(step, side), tile)
        return remote(
            part.at[span_of(slot), span],
            got.at[landing, :, span],
            t_send.at[side * n + k, step],
            t_recv.at[side * n + k, step],
            {"tensor": lax.rem(me + k, n)},
        )

    def compute(step, side):
        for load in loads(step, side):
            load.wait()
        first = column(step, side)
        added[...] = (
            contract_trailing_axis(rows_ref[:, :query_columns], query_buf[side])
            + contract_trailing_axis(
                rows_ref[:, query_columns : query_columns + key_value_columns],
                key_value_buf[side, 0],
            )
            + contract_trailing_axis(
                rows_ref[:, query_columns + key_value_columns :], key_value_buf[side, 1]
            )
        )

        @pl.when(lax.div(first, block) == me)
        def _():
            local_column = pl.multiple_of(first - me * block, tile)
            added[...] += jnp.dot(
                adapter_ref[...],
                down_ref[:, pl.ds(local_column, tile)],
                preferred_element_type=f32,
            )

        part[:, pl.ds(first, tile)] = added[...].astype(part.dtype)

        @pl.when(step + 1 < steps)
        def _():
            for load in loads(step + 1, side):
                load.start()

    def send(step, side):
        if n == 4:
            t_first(step, side, 0).start()
            t_first(step, side, 1).start()
        else:
            for k in range(1, n):
                t_direct(step, side, k, lax.rem(me + k, n), me).start()

    for i in range(nd):
        pltpu.make_async_copy(d_in[i].at[:, core], d_own[i], d_load.at[i]).wait()
        d_pair(i).wait_recv()
        for d in range(pairs):
            d_own[i][d] = (d_own[i][d].astype(f32) + d_sib[i][d].astype(f32)).astype(
                d_own[i].dtype
            )

    def d_copy(i, direction, slot, source):
        return remote(
            source,
            d_side[i].at[direction, slot],
            d_send.at[i, direction, slot],
            d_recv.at[i, direction, slot],
            (right, left)[direction],
        )

    def d_outer(j):
        for direction, d in ((0, pairs - 1 - j), (1, j)):

            @pl.when(spot == 0 if direction == 0 else spot == pairs - 1)
            def _(direction=direction, d=d):
                for i in range(nd):
                    d_copy(i, direction, j, d_own[i].at[d]).start()

    def d_inner(j):
        for direction, d in ((0, pairs - 1 - j), (1, j)):

            @pl.when(
                (spot > 0) & (spot < d) if direction == 0 else (spot < pairs - 1) & (spot > d)
            )
            def _(direction=direction, d=d):
                for i in range(nd):
                    here = d_side[i].at[direction, j]
                    d_copy(i, direction, j, here).wait_recv()
                    here[...] = (here[...].astype(f32) + d_own[i][d].astype(f32)).astype(
                        here.dtype
                    )
                    d_copy(i, direction, j, here).start()

    for j in range(pairs - 1):
        d_outer(j)

    def make(step, carry):
        compute(step, 0)
        pl.when(step > 0)(lambda: send(step - 1, 1))
        compute(step, 1)
        send(step, 0)
        return carry

    lax.fori_loop(0, steps, make, 0)
    send(steps - 1, 1)

    def forward(step, carry):
        for side in range(2):
            slot = (by_y, by_x)[side]
            span = pl.ds(pl.multiple_of(step * tile, tile), tile)
            t_first(step, side, 0).wait_recv()
            got[side, 0, :, span] = (
                got[side, 0, :, span].astype(f32)
                + part[span_of(slot), pl.ds(column(step, side), tile)].astype(f32)
            ).astype(got.dtype)
            t_second(step, side).start()
        return carry

    if pairs > 1:
        d_inner(0)
    if n == 4:
        lax.fori_loop(0, steps, forward, 0)
    for j in range(1, pairs - 1):
        d_inner(j)

    def close(step, carry):
        for side in range(2):
            here = pl.ds(column(step, side), tile)
            total_part = part[span_of(me), here].astype(f32)
            if n == 4:
                span = pl.ds(pl.multiple_of(step * tile, tile), tile)
                t_first(step, side, 1).wait_recv()
                t_second(step, side).wait_recv()
                total_part = total_part + got[side, 1, :, span].astype(f32)
                total_part = total_part + end[side, :, span].astype(f32)
                t_first(step, side, 0).wait_send()
                t_first(step, side, 1).wait_send()
                t_second(step, side).wait_send()
            else:
                for k in range(1, n):
                    source = lax.rem(me + n - k, n)
                    t_direct(step, side, k, me, source).wait_recv()
                    total_part = total_part + got[source, :, here].astype(f32)
                for k in range(1, n):
                    t_direct(step, side, k, lax.rem(me + k, n), me).wait_send()
            t_out[:, here] = total_part.astype(t_out.dtype)
        return carry

    lax.fori_loop(0, steps, close, 0)

    for i in range(nd):
        d_out[i][...] = d_own[i][spot].astype(f32)

        @pl.when(spot > 0)
        def _(i=i):
            slot = pairs - 1 - spot
            here = d_side[i].at[0, slot]
            d_copy(i, 0, slot, here).wait_recv()
            d_out[i][...] = d_out[i][...] + here[...].astype(f32)

        @pl.when(spot < pairs - 1)
        def _(i=i):
            here = d_side[i].at[1, spot]
            d_copy(i, 1, spot, here).wait_recv()
            d_out[i][...] = d_out[i][...] + here[...].astype(f32)

    for i in range(nd):
        d_pair(i).wait_send()
        for j in range(pairs - 1):
            for direction, d in ((0, pairs - 1 - j), (1, j)):
                pl.when(spot < d if direction == 0 else spot > d)(
                    lambda i=i, direction=direction, j=j: d_copy(
                        i, direction, j, d_side[i].at[direction, j]
                    ).wait_send()
                )


def finish_all(gradient_rows, adapter_rows, down, query_w, key_value_w, dp_arrays, collective_id):
    n, total = lax.axis_size("tensor"), lax.axis_size("dp")
    nd = len(dp_arrays)
    pairs = total // 2
    tokens, width = gradient_rows.shape[0], query_w.shape[0]
    rows, half = tokens // n, width // 2
    tile = min(512, half, width // n)
    steps = half // tile
    shaped = [a.reshape(pairs, 2, a.shape[0] // total, a.shape[1]) for a in dp_arrays]
    dma = pltpu.SemaphoreType.DMA
    kind = gradient_rows.dtype
    if n == 4:
        landing = [pltpu.VMEM((2, 2, rows, half), kind), pltpu.VMEM((2, rows, half), kind)]
        flows = 6
    else:
        landing = [pltpu.VMEM((n, rows, width), kind), pltpu.VMEM((16, 128), kind)]
        flows = 2 * n
    return pl.pallas_call(
        functools.partial(finish_kernel, n, total, tile, nd),
        out_shape=[jax.ShapeDtypeStruct((rows, width), kind)]
        + [jax.ShapeDtypeStruct(a.shape[2:], jnp.float32) for a in shaped],
        in_specs=[VMEM] * 3 + [ANY] * (2 + nd),
        out_specs=[VMEM] * (1 + nd),
        scratch_shapes=[
            pltpu.VMEM((tokens, width), kind),
            pltpu.VMEM((tokens, tile), jnp.float32),
            *landing,
            pltpu.VMEM((2, tile, query_w.shape[1]), kind),
            pltpu.VMEM((2, 2, tile, key_value_w.shape[2]), kind),
        ]
        + [pltpu.VMEM((pairs,) + a.shape[2:], a.dtype) for a in shaped]
        + [pltpu.VMEM((pairs,) + a.shape[2:], a.dtype) for a in shaped]
        + [pltpu.VMEM((2, max(pairs - 1, 1)) + a.shape[2:], a.dtype) for a in shaped]
        + [
            dma((2, 2)),
            dma((nd,)),
            dma((flows, steps)),
            dma((flows, steps)),
            dma((nd, 2, pairs)),
            dma((nd, 2, pairs)),
            dma((nd,)),
            dma((nd,)),
        ],
        compiler_params=pltpu.CompilerParams(
            collective_id=collective_id, has_side_effects=True, vmem_limit_bytes=VMEM_BYTES
        ),
        name="finish_all",
    )(gradient_rows, adapter_rows, down, query_w, key_value_w, *shaped)


adapter_scale = 2.0
rope_theta = 500000.0
masked_score = -1e30


def contract_trailing_axis(left, right):
    return lax.dot_general(
        left, right, (((1,), (1,)), ((), ())), preferred_element_type=jnp.float32
    )


def contract_leading_axis(left, right):
    return lax.dot_general(
        left, right, (((0,), (0,)), ((), ())), preferred_element_type=jnp.float32
    )


def token_tables(lengths, adapters, tok_total, adapter_overall_count):
    seq_ends = jnp.cumsum(lengths)
    seq_starts = seq_ends - lengths
    token_ids = jnp.arange(tok_total, dtype=jnp.int32)
    member = (
        (token_ids[:, None] >= seq_starts[None, :]) & (token_ids[:, None] < seq_ends[None, :])
    ).astype(jnp.int32)
    seq_index = jnp.sum(member * jnp.arange(lengths.shape[0], dtype=jnp.int32)[None, :], axis=1)
    position = token_ids - jnp.sum(member * seq_starts[None, :], axis=1)
    adapter_of = jnp.sum(member * adapters[None, :], axis=1)
    adapter_hot = adapter_of[:, None] == jnp.arange(adapter_overall_count, dtype=jnp.int32)[None, :]
    allowed = (seq_index[:, None] == seq_index[None, :]) & (
        token_ids[None, :] <= token_ids[:, None]
    )
    return (position, adapter_hot, allowed)


def rope_tables(position):
    half_dim = HEAD_SIZE // 2
    inverse = rope_theta ** (-(jnp.arange(half_dim, dtype=jnp.float32) * (2.0 / HEAD_SIZE)))
    angle = position.astype(jnp.float32)[:, None] * inverse[None, :]
    cosine_table = jnp.concatenate([jnp.cos(angle), jnp.cos(angle)], axis=1)
    sine_table = jnp.concatenate([jnp.sin(angle), jnp.sin(angle)], axis=1)
    return (cosine_table, sine_table)


def apply_rotation(vectors, cosine_table, sine_table):
    half_dim = HEAD_SIZE // 2
    turned = jnp.concatenate([-vectors[..., half_dim:], vectors[..., :half_dim]], axis=-1)
    return vectors * cosine_table[:, None, :] + turned * sine_table[:, None, :]


def choose_rank_rows(onehot_single, product, rank_width):
    shaped = product.reshape(product.shape[0], onehot_single.shape[1], rank_width)
    return jnp.sum(shaped * onehot_single[:, :, None], axis=1)


def expand_from_rank(onehot_halfprec, factors):
    return (onehot_halfprec[:, :, None] * factors[:, None, :]).reshape(
        factors.shape[0], onehot_halfprec.shape[1] * factors.shape[1]
    )


def attend(queries, rotated_keys, incoming_values, allowed):
    tok_total, head_count, _ = queries.shape
    group_count = rotated_keys.shape[1]
    per_group = head_count // group_count
    grouped = queries.reshape(tok_total, group_count, per_group, HEAD_SIZE)
    scores = jnp.einsum(
        "tgpe,sge->gpts", grouped, rotated_keys, preferred_element_type=jnp.float32
    ) * HEAD_SIZE ** (-0.5)
    scores = jnp.where(allowed[None, None], scores, masked_score)
    peak = jnp.max(scores, axis=-1, keepdims=True)
    expped = jnp.exp(scores - peak)
    probs = expped / jnp.sum(expped, axis=-1, keepdims=True)
    probs_bf = probs.astype(jnp.bfloat16)
    blended_output = jnp.einsum(
        "gpts,sge->tgpe", probs_bf, incoming_values, preferred_element_type=jnp.float32
    )
    return (
        blended_output.reshape(tok_total, head_count * HEAD_SIZE).astype(jnp.bfloat16),
        probs,
        probs_bf,
    )


def attend_back(queries, rotated_keys, incoming_values, probs, probs_bf, blended_gradient):
    tok_total, head_count, _ = queries.shape
    group_count = rotated_keys.shape[1]
    per_group = head_count // group_count
    incoming_gradient = blended_gradient.reshape(tok_total, group_count, per_group, HEAD_SIZE)
    grad_probs = jnp.einsum(
        "tgpe,sge->gpts", incoming_gradient, incoming_values, preferred_element_type=jnp.float32
    )
    grad_values = jnp.einsum(
        "gpts,tgpe->sge", probs_bf, incoming_gradient, preferred_element_type=jnp.float32
    )
    inner = jnp.sum(grad_probs * probs, axis=-1, keepdims=True)
    grad_scores = (probs * (grad_probs - inner) * HEAD_SIZE ** (-0.5)).astype(jnp.bfloat16)
    grouped = queries.reshape(tok_total, group_count, per_group, HEAD_SIZE)
    grad_queries = jnp.einsum(
        "gpts,sge->tgpe", grad_scores, rotated_keys, preferred_element_type=jnp.float32
    )
    grad_keys = jnp.einsum(
        "gpts,tgpe->sge", grad_scores, grouped, preferred_element_type=jnp.float32
    )
    return (grad_queries.reshape(tok_total, head_count, HEAD_SIZE), grad_keys, grad_values)


def local(
    hidden_in,
    out_grad,
    seq_lengths,
    seq_adapter,
    query_weight,
    key_value_weight,
    output_weight,
    a_in,
    b_query,
    b_key_value,
    output_down_factor,
    output_up_factor,
):
    mesh_parts = lax.axis_size("tensor")
    own_slot = lax.axis_index("tensor")
    tok_rows = hidden_in.shape[0]
    tok_total = tok_rows * mesh_parts
    full_width = hidden_in.shape[1]
    narrow_cast = full_width // mesh_parts
    adapter_rank_rows = output_down_factor.shape[1]
    rank_piece = output_up_factor.shape[1]
    query_columns = query_weight.shape[1]
    key_value_columns = key_value_weight.shape[2]
    (
        projected,
        gathered,
        input_down_every,
        query_up_every,
        key_value_up_every,
        output_down_every,
        b_out_all,
    ) = gather_all(
        [hidden_in],
        [a_in, b_query, b_key_value, output_down_factor, output_up_factor],
        query_weight,
        key_value_weight,
        0,
    )
    out_grad, gathered = lax.optimization_barrier((out_grad, gathered))
    incoming_gradient = lax.all_gather(out_grad, "tensor", axis=0, tiled=True)
    adapter_overall_count = input_down_every.shape[0]
    position, adapter_hot, allowed = token_tables(
        seq_lengths[0], seq_adapter[0], tok_total, adapter_overall_count
    )
    onehot_single = adapter_hot.astype(jnp.float32)
    onehot_halfprec = adapter_hot.astype(jnp.bfloat16)
    cosine_table, sine_table = rope_tables(position)
    input_down_flattened = input_down_every.reshape(
        adapter_overall_count * 3 * adapter_rank_rows, narrow_cast
    )
    query_up_flattened = query_up_every.reshape(
        adapter_overall_count * adapter_rank_rows, query_columns
    )
    key_up_flattened = key_value_up_every[:, 0].reshape(
        adapter_overall_count * adapter_rank_rows, key_value_columns
    )
    value_up_flattened = key_value_up_every[:, 1].reshape(
        adapter_overall_count * adapter_rank_rows, key_value_columns
    )
    output_down_flattened = output_down_every.reshape(
        adapter_overall_count * adapter_rank_rows, query_columns
    )
    output_up_flattened = b_out_all.reshape(adapter_overall_count * rank_piece, full_width)
    col_start = own_slot * narrow_cast
    local_columns = lax.dynamic_slice_in_dim(gathered, col_start, narrow_cast, 1)
    rank_partial_sum = choose_rank_rows(
        onehot_single,
        contract_trailing_axis(local_columns, input_down_flattened),
        3 * adapter_rank_rows,
    )
    input_rank_rows = small_sum(rank_partial_sum, 1).astype(jnp.bfloat16)
    adapter_query_delta = expand_from_rank(onehot_halfprec, input_rank_rows[:, :adapter_rank_rows])
    adapter_key_delta = expand_from_rank(
        onehot_halfprec, input_rank_rows[:, adapter_rank_rows : 2 * adapter_rank_rows]
    )
    adapter_value_delta = expand_from_rank(
        onehot_halfprec, input_rank_rows[:, 2 * adapter_rank_rows :]
    )
    query_before_rotation = projected[:, :query_columns] + adapter_scale * jnp.dot(
        adapter_query_delta, query_up_flattened, preferred_element_type=jnp.float32
    )
    key_before_rotation = projected[
        :, query_columns : query_columns + key_value_columns
    ] + adapter_scale * jnp.dot(
        adapter_key_delta, key_up_flattened, preferred_element_type=jnp.float32
    )
    value_projected = projected[:, query_columns + key_value_columns :] + adapter_scale * jnp.dot(
        adapter_value_delta, value_up_flattened, preferred_element_type=jnp.float32
    )
    queries = apply_rotation(
        query_before_rotation.reshape(tok_total, query_columns // HEAD_SIZE, HEAD_SIZE),
        cosine_table,
        sine_table,
    ).astype(jnp.bfloat16)
    rotated_keys = apply_rotation(
        key_before_rotation.reshape(tok_total, key_value_columns // HEAD_SIZE, HEAD_SIZE),
        cosine_table,
        sine_table,
    ).astype(jnp.bfloat16)
    incoming_values = value_projected.reshape(
        tok_total, key_value_columns // HEAD_SIZE, HEAD_SIZE
    ).astype(jnp.bfloat16)
    blended_output, probs, probs_bf = attend(queries, rotated_keys, incoming_values, allowed)
    output_partial_sum = choose_rank_rows(
        onehot_single,
        contract_trailing_axis(blended_output, output_down_flattened),
        adapter_rank_rows,
    )
    grad_part = (
        adapter_scale
        * choose_rank_rows(
            onehot_single,
            contract_trailing_axis(incoming_gradient, output_up_flattened),
            rank_piece,
        )
    ).astype(jnp.bfloat16)
    placed_part = lax.dynamic_update_slice_in_dim(
        jnp.zeros((tok_total, adapter_rank_rows), jnp.float32),
        grad_part.astype(jnp.float32),
        own_slot * rank_piece,
        1,
    )
    both_ranks = small_sum(jnp.concatenate([output_partial_sum, placed_part], axis=1), 2).astype(
        jnp.bfloat16
    )
    output_rank_rows = both_ranks[:, :adapter_rank_rows]
    output_rank_gradient = both_ranks[:, adapter_rank_rows:]
    adapter_output_delta = expand_from_rank(
        onehot_halfprec,
        lax.dynamic_slice_in_dim(output_rank_rows, own_slot * rank_piece, rank_piece, 1),
    )
    adapter_row_values = adapter_output_delta
    attn_out = lax.psum_scatter(
        (
            jnp.dot(blended_output, output_weight, preferred_element_type=jnp.float32)
            + adapter_scale
            * jnp.dot(adapter_row_values, output_up_flattened, preferred_element_type=jnp.float32)
        ).astype(jnp.bfloat16),
        "tensor",
        scatter_dimension=0,
        tiled=True,
    )
    output_up_gradient = (
        adapter_scale * contract_leading_axis(adapter_output_delta, incoming_gradient)
    ).reshape(adapter_overall_count, rank_piece, full_width)
    adapter_output_gradient = expand_from_rank(onehot_halfprec, output_rank_gradient)
    blended_gradient = (
        contract_trailing_axis(incoming_gradient, output_weight)
        + jnp.dot(
            adapter_output_gradient, output_down_flattened, preferred_element_type=jnp.float32
        )
    ).astype(jnp.bfloat16)
    output_down_gradient = contract_leading_axis(adapter_output_gradient, blended_output).reshape(
        adapter_overall_count, adapter_rank_rows, query_columns
    )
    half = jnp.bfloat16
    wide = lambda grad: grad.reshape(-1, grad.shape[-1]).astype(half)
    early = jnp.concatenate(
        [
            output_down_gradient.astype(half),
            output_up_gradient.astype(half).reshape(adapter_overall_count, -1, query_columns),
        ],
        axis=1,
    )
    summed_early = lax.psum_scatter(early, "dp", scatter_dimension=0, tiled=True).astype(
        jnp.float32
    )
    summed_a_out = summed_early[:, :adapter_rank_rows]
    summed_b_out = summed_early[:, adapter_rank_rows:].reshape(output_up_factor.shape)
    grad_queries, grad_keys, grad_values = attend_back(
        queries, rotated_keys, incoming_values, probs, probs_bf, blended_gradient
    )
    query_gradient_rows = (
        apply_rotation(grad_queries, cosine_table, -sine_table)
        .reshape(tok_total, query_columns)
        .astype(jnp.bfloat16)
    )
    key_gradient_rows = (
        apply_rotation(grad_keys, cosine_table, -sine_table)
        .reshape(tok_total, key_value_columns)
        .astype(jnp.bfloat16)
    )
    value_gradient_rows = grad_values.reshape(tok_total, key_value_columns).astype(jnp.bfloat16)
    backward_partial_sum = jnp.concatenate(
        [
            choose_rank_rows(
                onehot_single,
                contract_trailing_axis(query_gradient_rows, query_up_flattened),
                adapter_rank_rows,
            ),
            choose_rank_rows(
                onehot_single,
                contract_trailing_axis(key_gradient_rows, key_up_flattened),
                adapter_rank_rows,
            ),
            choose_rank_rows(
                onehot_single,
                contract_trailing_axis(value_gradient_rows, value_up_flattened),
                adapter_rank_rows,
            ),
        ],
        axis=1,
    )
    input_rank_gradient = (adapter_scale * small_sum(backward_partial_sum, 3)).astype(
        jnp.bfloat16
    )
    query_up_gradient = (
        adapter_scale * contract_leading_axis(adapter_query_delta, query_gradient_rows)
    ).reshape(adapter_overall_count, adapter_rank_rows, query_columns)
    key_up_gradient = (
        adapter_scale * contract_leading_axis(adapter_key_delta, key_gradient_rows)
    ).reshape(adapter_overall_count, adapter_rank_rows, key_value_columns)
    value_up_gradient = (
        adapter_scale * contract_leading_axis(adapter_value_delta, value_gradient_rows)
    ).reshape(adapter_overall_count, adapter_rank_rows, key_value_columns)
    grad_b_kv = jnp.stack([key_up_gradient, value_up_gradient], axis=1)
    adapter_input_gradient = expand_from_rank(onehot_halfprec, input_rank_gradient)
    input_down_gradient = contract_leading_axis(adapter_input_gradient, local_columns).reshape(
        adapter_overall_count, 3 * adapter_rank_rows, narrow_cast
    )
    input_grad, *summed = finish_all(
        jnp.concatenate([query_gradient_rows, key_gradient_rows, value_gradient_rows], axis=1),
        adapter_input_gradient,
        input_down_flattened,
        query_weight,
        key_value_weight,
        [
            wide(input_down_gradient),
            wide(query_up_gradient),
            wide(grad_b_kv),
        ],
        4,
    )
    summed_a_in, summed_b_query, summed_b_kv = [
        s.reshape(factor.shape)
        for s, factor in zip(summed, (a_in, b_query, b_key_value))
    ]
    return (
        attn_out,
        input_grad,
        summed_a_in,
        summed_b_query,
        summed_b_kv,
        summed_a_out,
        summed_b_out,
    )


def solution(mesh):
    in_specs = (
        P(("dp", "tensor"), None),
        P(("dp", "tensor"), None),
        P("dp", None),
        P("dp", None),
        P(None, "tensor"),
        P(None, None, "tensor"),
        P("tensor", None),
        P("dp", None, "tensor"),
        P("dp", None, "tensor"),
        P("dp", None, None, "tensor"),
        P("dp", None, "tensor"),
        P("dp", "tensor", None),
    )
    out_specs = (
        P(("dp", "tensor"), None),
        P(("dp", "tensor"), None),
        P("dp", None, "tensor"),
        P("dp", None, "tensor"),
        P("dp", None, None, "tensor"),
        P("dp", None, "tensor"),
        P("dp", "tensor", None),
    )
    return jax.shard_map(local, mesh=mesh, in_specs=in_specs, out_specs=out_specs, check_vma=False)
```
